128 devices in a mesh: row: 8 (over z_hi, y), col: 16 (over z_lo, x, core).
Axes of the slice: x: 4, y: 4, z: 4 (z_hi: 2, z_lo: 2; z = z_hi * 2 + z_lo), core: 2. Of those that a mesh axis runs over, the one named last changes fastest.
Arguments:
- node_coords: float32 [3, 131072], P(None, ('row', 'col')), may hold values from -0.08 to 66.08, as said below
- tet_nodes: int32 [4, 864000], P(None, ('row', 'col')), may hold values from -1 to 1535, as said below
- bnd_nodes: int32 [55808], P(('row', 'col')), may hold values from -1 to 1023, as said below
- reaction: float32 [131072], P(('row', 'col')), may hold values from 0.05 to 0.5
- load: float32 [131072], P(('row', 'col')), may hold values from -8 to 8
- area_normal: float32 [3, 55808], P(None, ('row', 'col')), may hold values from -2 to 2
Outputs:
- solution: float32 [131072], P(('row', 'col'))
- demag_potential: float32 [55808], P(('row', 'col'))
The draws below stay inside these ranges and needn't reach their ends.
Inputs may be any that keep to these rules, and one draw needn't show every extreme that they name: `tet_nodes`: own node n of a partition lies in its layer n // 256; layers run along the grain, partitions of a grain follow their col index. Each column lists the corners of one tetrahedron as indices into the partition's ghost-extended list (see the steps); each lattice cell of a grain is split into six tetrahedra around one of its main diagonals, the same on every partition that lists them; every tetrahedron of the grain that has an own node of the partition as a corner stands exactly once on that partition; -1 marks an empty column, all four entries then -1. Tetrahedra have volumes bounded away from zero. `bnd_nodes`: each own node on the surface of its grain stands in exactly one slot of its partition; other slots hold -1. The partitions at the two ends of a grain fill all 436 slots. `node_coords`: node positions of the grains' meshes.
All inputs are finite; a program needn't handle non-finite values.
Results may differ from the reference program's by a relative error of at most 0.0003.
Values sent between devices are 32-bit elements; how exact they have to be, the bound alone decides.
A program may use at most 128 MiB of HBM per device.

```python
import math
from functools import partial
import jax
import jax.numpy as jnp
import numpy as np
from jax import lax

QS = 16
LAYERS = 4
ITERS = 3
GRAINS = 8
CHAIN = 16
PARTITIONS = 128
NODES_DEV = 1024
ELEMS_DEV = 6750
BND_DEV = 436


def kuhn_table():
    paths = []
    for axis_order in [(0, 1, 2), (0, 2, 1), (1, 0, 2), (1, 2, 0), (2, 0, 1), (2, 1, 0)]:
        corner_now = [0, 0, 0]
        walk = [list(corner_now)]
        for axis_pick in axis_order:
            corner_now = list(corner_now)
            corner_now[axis_pick] = 1
            walk.append(list(corner_now))
        paths.append(walk)
    return np.array(paths, dtype=np.int32)


def node_layout():
    square = QS * QS
    node_ids = jnp.arange(NODES_DEV)
    return (node_ids // square, node_ids % square // QS, node_ids % QS)


def draw_node_coords(key, part):
    node_layer, node_row, node_col = node_layout()
    part_ids = jnp.arange(PARTITIONS)
    grain_ids = part_ids // CHAIN
    link_ids = part_ids % CHAIN
    coord_x = (grain_ids % 4 * (QS + 1))[:, None] + node_row[None, :]
    coord_y = (grain_ids // 4 * (QS + 1))[:, None] + node_col[None, :]
    coord_z = (link_ids * LAYERS)[:, None] + node_layer[None, :]
    lattice = jnp.stack([coord_x, coord_y, coord_z]).astype(jnp.float32).reshape(3, PARTITIONS * NODES_DEV)
    jitter = jax.random.uniform(key, lattice.shape, minval=-0.08, maxval=0.08)
    return lattice + jitter


def draw_tet_nodes(key, part):
    table = jnp.asarray(kuhn_table())
    square = QS * QS
    cell_ids = jnp.arange((LAYERS + 1) * (QS - 1) * (QS - 1))
    cell_layer = cell_ids // ((QS - 1) * (QS - 1))
    cell_row = cell_ids // (QS - 1) % (QS - 1)
    cell_col = cell_ids % (QS - 1)
    layer_of = jnp.repeat(cell_layer, 6)
    flips = jax.random.randint(jax.random.fold_in(key, 7), (GRAINS, CHAIN * LAYERS + 1, QS - 1, QS - 1), 0, 8).astype(jnp.int32)

    def one_part(part_index):
        grain_id = part_index // CHAIN
        link_id = part_index % CHAIN
        global_layer = jnp.clip(link_id * LAYERS + cell_layer, 0, CHAIN * LAYERS).astype(jnp.int32)
        cell_flip = flips[grain_id, global_layer, cell_row, cell_col]
        bit_row = (jnp.right_shift(cell_flip, 0) % 2)[:, None, None]
        bit_col = (jnp.right_shift(cell_flip, 1) % 2)[:, None, None]
        bit_layer = (jnp.right_shift(cell_flip, 2) % 2)[:, None, None]
        corner_row = cell_row[:, None, None] + jnp.abs(table[None, :, :, 0] - bit_row)
        corner_col = cell_col[:, None, None] + jnp.abs(table[None, :, :, 1] - bit_col)
        corner_layer = cell_layer[:, None, None] + jnp.abs(table[None, :, :, 2] - bit_layer)
        ext_index = corner_layer * square + corner_row * QS + corner_col
        corners = ext_index.reshape(-1, 4).T
        usable = jnp.logical_and(jnp.logical_or(link_id > 0, layer_of > 0), jnp.logical_or(link_id < CHAIN - 1, layer_of < LAYERS))
        filled = jnp.where(usable[None, :], corners, -1)
        ordering = jax.random.permutation(jax.random.fold_in(key, part_index), ELEMS_DEV)
        return filled[:, ordering]
    blocks = jax.vmap(one_part)(jnp.arange(PARTITIONS))
    return blocks.transpose(1, 0, 2).reshape(4, PARTITIONS * ELEMS_DEV).astype(jnp.int32)


def boundary_slots(key):
    base = jax.random.fold_in(key, 101)
    node_layer, node_row, node_col = node_layout()
    on_side = (node_row == 0) | (node_row == QS - 1) | (node_col == 0) | (node_col == QS - 1)

    def one_part(part_index):
        link_id = part_index % CHAIN
        bottom = (link_id == 0) & (node_layer == 0)
        top_face = (link_id == CHAIN - 1) & (node_layer == LAYERS - 1)
        surface = on_side | bottom | top_face
        ranking = jax.random.permutation(jax.random.fold_in(base, 2 * part_index), NODES_DEV)
        scores = jnp.where(surface, 0, NODES_DEV) + ranking
        chosen = jnp.argsort(scores)[:BND_DEV]
        listed = jnp.where(surface[chosen], chosen, -1)
        shuffle = jax.random.permutation(jax.random.fold_in(base, 2 * part_index + 1), BND_DEV)
        return listed[shuffle]
    return jax.vmap(one_part)(jnp.arange(PARTITIONS)).astype(jnp.int32)


def draw_bnd_nodes(key, part):
    return boundary_slots(key).reshape(-1).astype(jnp.int32)


def draw_area_normal(key, part):
    square = QS * QS
    slots = boundary_slots(key)
    node_ids = jnp.maximum(slots, 0)
    node_layer = node_ids // square
    node_row = node_ids % square // QS
    node_col = node_ids % QS
    link_ids = (jnp.arange(PARTITIONS) % CHAIN)[:, None]
    along = link_ids * LAYERS + node_layer
    top_end = CHAIN * LAYERS - 1
    end_row = (node_row == 0) | (node_row == QS - 1)
    end_col = (node_col == 0) | (node_col == QS - 1)
    end_along = (along == 0) | (along == top_end)
    half_row = jnp.where(end_row, 0.5, 1.0)
    half_col = jnp.where(end_col, 0.5, 1.0)
    half_along = jnp.where(end_along, 0.5, 1.0)
    normal_x = (jnp.where(node_row == QS - 1, 1.0, 0.0) - jnp.where(node_row == 0, 1.0, 0.0)) * half_col * half_along
    normal_y = (jnp.where(node_col == QS - 1, 1.0, 0.0) - jnp.where(node_col == 0, 1.0, 0.0)) * half_row * half_along
    normal_z = (jnp.where(along == top_end, 1.0, 0.0) - jnp.where(along == 0, 1.0, 0.0)) * half_row * half_col
    outward = jnp.stack([normal_x, normal_y, normal_z]).astype(jnp.float32)
    key_area = jax.random.fold_in(key, 201)
    key_tilt = jax.random.fold_in(key, 202)
    factor = jax.random.uniform(key_area, (PARTITIONS, BND_DEV), minval=0.6, maxval=1.4)
    tilt = 0.3 * jnp.clip(jax.random.normal(key_tilt, (3, PARTITIONS, BND_DEV)), -1.5, 1.5)
    return (outward * factor[None] + tilt).reshape(3, PARTITIONS * BND_DEV).astype(jnp.float32)


def draw_load(key, part):
    node_layer, node_row, node_col = node_layout()
    part_ids = jnp.arange(PARTITIONS)
    grain_ids = part_ids // CHAIN
    link_ids = part_ids % CHAIN
    along = ((link_ids * LAYERS)[:, None] + node_layer[None, :]).astype(jnp.float32) / (CHAIN * LAYERS)
    grain_sign = jnp.where(jax.random.uniform(jax.random.fold_in(key, 1), (GRAINS,)) < 0.5, -1.0, 1.0)
    phase = jax.random.uniform(jax.random.fold_in(key, 3), (GRAINS,), minval=0.0, maxval=2.0 * jnp.pi)
    level = jax.random.uniform(jax.random.fold_in(key, 2), (GRAINS,), minval=1.5, maxval=2.5)
    wave = jnp.sin(1.5 * jnp.pi * along + phase[grain_ids][:, None])
    smooth = (grain_sign * level)[grain_ids][:, None] * (1.0 + 0.4 * wave)
    rough = jnp.clip(jax.random.normal(jax.random.fold_in(key, 4), (PARTITIONS, NODES_DEV)), -4.0, 4.0)
    return (smooth + rough).reshape(PARTITIONS * NODES_DEV).astype(jnp.float32)


def block_scale(own_key, dims, pieces, smallest, largest):
    gain, own = 1.0, jax.random.fold_in(own_key, 6)
    for dim, blocks in pieces:
        steps = jnp.exp(jax.random.uniform(jax.random.fold_in(own, dim), (blocks,), jnp.float32, smallest / len(pieces), largest / len(pieces)))
        gain = gain * jnp.repeat(steps, dims[dim] // blocks).reshape([-1 if axis == dim else 1 for axis in range(len(dims))])
    return gain


def setup_inputs(seed: int = 0) -> dict:
    key_list = jax.random.split(jax.random.key(seed), 7)
    node_coords = draw_node_coords(jax.random.fold_in(key_list[6], 71), 0)
    tet_nodes = draw_tet_nodes(jax.random.fold_in(key_list[6], 71), 0)
    bnd_nodes = draw_bnd_nodes(jax.random.fold_in(key_list[6], 71), 0)
    reaction = jnp.clip(jnp.exp(math.log(0.5) - 2.3025851 * jax.random.uniform(key_list[3], (PARTITIONS * NODES_DEV,), jnp.float32) ** block_scale(key_list[3], (PARTITIONS * NODES_DEV,), ((0, 128),), -0.2, 0.2)), 0.05, 0.5)
    load = draw_load(jax.random.fold_in(key_list[6], 71), 0)
    area_normal = draw_area_normal(jax.random.fold_in(key_list[6], 71), 0)
    return dict(node_coords=node_coords, tet_nodes=tet_nodes, bnd_nodes=bnd_nodes, reaction=reaction, load=load, area_normal=area_normal)


def cross_product(left_vec, right_vec):
    return jnp.stack([left_vec[1] * right_vec[2] - left_vec[2] * right_vec[1], left_vec[2] * right_vec[0] - left_vec[0] * right_vec[2], left_vec[0] * right_vec[1] - left_vec[1] * right_vec[0]])

def element_matrices(ext_coords, corners):
    present = corners[0] >= 0
    corner_ids = jnp.maximum(corners, 0)
    vertex_zero = ext_coords[:, corner_ids[0]]
    edge_one = ext_coords[:, corner_ids[1]] - vertex_zero
    edge_two = ext_coords[:, corner_ids[2]] - vertex_zero
    edge_three = ext_coords[:, corner_ids[3]] - vertex_zero
    normal_one = cross_product(edge_two, edge_three)
    normal_two = cross_product(edge_three, edge_one)
    normal_three = cross_product(edge_one, edge_two)
    normal_zero = -(normal_one + normal_two + normal_three)
    volume_six = lax.optimization_barrier(jnp.sum(edge_one * normal_one, axis=0))
    safe_volume = jnp.abs(jnp.where(present, volume_six, 1.0))
    weights = jnp.where(present, 1.0 / (6.0 * safe_volume), 0.0)
    normals = jnp.stack([normal_zero, normal_one, normal_two, normal_three])
    stiffness = lax.optimization_barrier(jnp.sum(normals[:, None] * normals[None, :], axis=2)) * weights
    return (stiffness, corner_ids)

def assemble(values, corner_ids, ext_len, own_count):
    accumulated = jnp.zeros((ext_len,), values.dtype).at[corner_ids.reshape(-1)].add(values.reshape(-1))
    margin = (ext_len - own_count) // 2
    return accumulated[margin:margin + own_count]

def pick_corners(extended, corner_ids):
    return extended[corner_ids]

def pick_columns(matrix, column_ids):
    return matrix[:, column_ids]

def tile_sum(targets, sources):
    delta_x = targets[0][:, None] - sources[0][None, :]
    delta_y = targets[1][:, None] - sources[1][None, :]
    delta_z = targets[2][:, None] - sources[2][None, :]
    distance = delta_x * delta_x + delta_y * delta_y + delta_z * delta_z + 0.25
    numerator = delta_x * sources[3][None, :] + delta_y * sources[4][None, :] + delta_z * sources[5][None, :]
    inverse = lax.rsqrt(distance)
    return lax.optimization_barrier(jnp.sum(numerator * inverse * inverse * inverse, axis=1)) * (0.25 / math.pi)

def ghosts(field):
    square = QS * QS
    leading = field.shape[:-1]
    blocks = field.reshape(leading + (GRAINS, CHAIN, NODES_DEV))
    zero_rim = jnp.zeros(leading + (GRAINS, 1, square), field.dtype)
    lower_rim = jnp.concatenate([zero_rim, blocks[..., :-1, NODES_DEV - square:]], axis=-2)
    upper_rim = jnp.concatenate([blocks[..., 1:, :square], zero_rim], axis=-2)
    extended = jnp.concatenate([lower_rim, blocks, upper_rim], axis=-1)
    return extended.reshape(leading + (PARTITIONS, NODES_DEV + 2 * square))

def reference(node_coords, tet_nodes, bnd_nodes, reaction, load, area_normal):
    ext_len = NODES_DEV + 2 * QS * QS
    react_parts = reaction.reshape(PARTITIONS, NODES_DEV)
    stiff_all, ids_all = jax.vmap(element_matrices, in_axes=(1, 1))(ghosts(node_coords), tet_nodes.reshape(4, PARTITIONS, ELEMS_DEV))
    place = jax.vmap(partial(assemble, ext_len=ext_len, own_count=NODES_DEV))
    diag_terms = jnp.stack([stiff_all[:, k, k] for k in range(4)], axis=1)
    diagonal = (react_parts + place(diag_terms, ids_all)).reshape(-1)

    def operate(field):
        extended = ghosts(field)
        corner_vals = jax.vmap(pick_corners)(extended, ids_all)
        products = lax.optimization_barrier(jnp.sum(stiff_all * corner_vals[:, None], axis=2))
        return (react_parts * field.reshape(PARTITIONS, NODES_DEV) + place(products, ids_all)).reshape(-1)
    solution = jnp.zeros_like(load)
    residual = load
    precond = residual / diagonal
    direction = precond
    rz_now = jnp.sum(residual * precond)
    for iteration in range(ITERS):
        image = operate(direction)
        step_size = rz_now / jnp.sum(direction * image)
        solution = solution + step_size * direction
        residual = residual - step_size * image
        if iteration + 1 < ITERS:
            precond = residual / diagonal
            rz_next = jnp.sum(residual * precond)
            direction = precond + rz_next / rz_now * direction
            rz_now = rz_next
    live_mask = (bnd_nodes >= 0).astype(jnp.float32)
    slot_ids = jnp.maximum(bnd_nodes, 0).reshape(PARTITIONS, BND_DEV)
    positions = jax.vmap(pick_columns, in_axes=(1, 0), out_axes=1)(node_coords.reshape(3, PARTITIONS, NODES_DEV), slot_ids).reshape(3, -1) * live_mask[None, :]
    traces = jax.vmap(pick_corners)(solution.reshape(PARTITIONS, NODES_DEV), slot_ids).reshape(-1) * live_mask
    weighted = area_normal * traces[None, :]
    sources = jnp.concatenate([positions, weighted], axis=0)

    def block_sum(target_block):
        return tile_sum(target_block, sources)
    target_blocks = positions.reshape(3, PARTITIONS, BND_DEV).transpose(1, 0, 2)
    row_sums = lax.map(block_sum, target_blocks).reshape(-1)
    demag_potential = live_mask * (-0.5 * traces + row_sums)
    return (solution, demag_potential)
```

```python
import functools
import math

import jax
import jax.numpy as jnp
from jax import lax
from jax.experimental import pallas as pl
from jax.experimental.pallas import tpu as pltpu
from jax.sharding import PartitionSpec as P

ITERS = 3
LANES = 128
SLOTS = 512
F32 = jnp.float32
BF16 = jnp.bfloat16
MESH = pl.DeviceIdType.MESH
VMEM = pl.BlockSpec(memory_space=pltpu.VMEM)
CHUNK = 2048
PAIRS = [(a, b) for a in range(4) for b in range(a, 4)]


def place():
    row, col = lax.axis_index("row"), lax.axis_index("col")
    z_hi, y = row // 4, row % 4
    z_lo, g = col // 8, col % 8
    return row, col, z_hi, y, z_lo, g


def peers():
    row, col, z_hi, y, z_lo, g = place()
    out = [(row, z_lo * 8 + (g + j) % 8) for j in range(1, 8)]
    out += [(z_hi * 4 + (y + j) % 4, col) for j in range(1, 4)]
    z = z_hi * 2 + z_lo
    for j in range(1, 4):
        other = (z + j) % 4
        out.append(((other // 2) * 4 + y, (other % 2) * 8 + g))
    return out


def lane_pick(table, low):
    return jnp.take_along_axis(table, low, axis=1, mode="promise_in_bounds")


def pick(rows, ids):
    low = ids & (LANES - 1)
    high = ids >> 7
    out = jnp.zeros(ids.shape, F32)
    for r, row in enumerate(rows):
        out = jnp.where(high == r, lane_pick(row, low), out)
    return out


def pieces(v):
    one = v.astype(BF16).astype(F32)
    rest = v - one
    two = rest.astype(BF16).astype(F32)
    return one, two, rest - two


def cross(u, v):
    return (
        u[1] * v[2] - u[2] * v[1],
        u[2] * v[0] - u[0] * v[2],
        u[0] * v[1] - u[1] * v[0],
    )


def dot3(u, v):
    return u[0] * v[0] + u[1] * v[1] + u[2] * v[2]


def chain_kernel(
    tet_ref, nc_ref, bnd_ref, an_ref, rea_ref, load_ref,
    sol_ref, g_ref, t_ref,
    ids, ext_c, ext_v, onehot, spread, stiff, vals, slots,
    red_a, red_y, red_z,
    halo_s, halo_r, red_s, red_r, all_s, all_r,
):
    row, col, z_hi, y, z_lo, g = place()
    z = z_hi * 2 + z_lo
    others = peers()
    before, after = (row, (col + 15) % 16), (row, (col + 1) % 16)
    elems = tet_ref.shape[1]
    count = bnd_ref.shape[1]
    tet_rows = ids.shape[1]

    barrier = pltpu.get_barrier_semaphore()
    for who in others + [before, after]:
        pl.semaphore_signal(barrier, inc=1, device_id=who, device_id_type=MESH)

    def send(src, dst, ssem, rsem, who):
        copy = pltpu.make_async_remote_copy(
            src_ref=src, dst_ref=dst, send_sem=ssem, recv_sem=rsem,
            device_id=who, device_id_type=MESH,
        )
        copy.start()
        return copy

    def halo(buf, k):
        return [
            send(buf.at[pl.ds(2, 2)], buf.at[pl.ds(10, 2)], halo_s.at[k, 0], halo_r.at[k, 0], before),
            send(buf.at[pl.ds(8, 2)], buf.at[pl.ds(0, 2)], halo_s.at[k, 1], halo_r.at[k, 1], after),
        ]

    def gather_stage(buf, k, stage):
        if stage == 0:
            part, first, last = buf.at[z_hi, y, z_lo, g], 0, 7
        elif stage == 1:
            part, first, last = buf.at[z_hi, y, z_lo], 7, 10
        else:
            part, first, last = buf.at[z_hi, :, z_lo], 10, 13
        return [send(part, part, all_s.at[k, j], all_r.at[k, j], others[j]) for j in range(first, last)]

    def finish(copies):
        for copy in copies:
            copy.wait()

    def reduce_all(u, v, k):
        for buf, mine, size, first in ((red_a, g, 8, 0), (red_y, y, 4, 7), (red_z, z, 4, 10)):
            here = buf.at[k]
            here[mine, 0] = u
            here[mine, 1] = v
            part = here.at[mine]
            finish([
                send(part, part, red_s.at[k, first + j], red_r.at[k, first + j], others[first + j])
                for j in range(size - 1)
            ])
            u, v = here[0, 0], here[0, 1]
            for i in range(1, size):
                u, v = u + here[i, 0], v + here[i, 1]
        return jnp.sum(u, keepdims=True), jnp.sum(v, keepdims=True)

    for s in range(8):
        for k in range(3):
            ext_c[2 + s, pl.ds(k, 1), :] = nc_ref[pl.ds(k, 1), pl.ds(s * LANES, LANES)]
        ext_c[2 + s, pl.ds(3, 5), :] = jnp.zeros((5, LANES), F32)

    slots[...] = jnp.full(slots.shape, -1, jnp.int32)
    for j in range(SLOTS // LANES):
        width = min(LANES, count - j * LANES)
        slots[pl.ds(j, 1), pl.ds(0, width)] = bnd_ref[:, pl.ds(j * LANES, width)]
    slot_ids = slots[...]
    live = jnp.where(slot_ids >= 0, 1.0, 0.0)
    mine = g_ref.at[z_hi, y, z_lo, g]
    mine[...] = jnp.zeros((8, SLOTS), F32)
    for k in range(3):
        tables = [jnp.broadcast_to(ext_c[2 + s, pl.ds(k, 1), :], (8, LANES)) for s in range(8)]
        spot = pick(tables, slot_ids)
        for j in range(SLOTS // LANES):
            mine[pl.ds(k, 1), pl.ds(j * LANES, LANES)] = spot[j : j + 1, :]
        mine[pl.ds(3 + k, 1), pl.ds(0, count)] = an_ref[pl.ds(k, 1), :]
    for j in range(SLOTS // LANES):
        mine[pl.ds(6, 1), pl.ds(j * LANES, LANES)] = live[j : j + 1, :]

    pl.semaphore_wait(barrier, len(others) + 2)
    coords_sent = halo(ext_c, 0)
    static_sent = gather_stage(g_ref, 0, 0)

    full = elems // LANES
    for a in range(4):
        ids[a, pl.ds(full // 8 * 8, tet_rows - full // 8 * 8), :] = jnp.full(
            (tet_rows - full // 8 * 8, LANES), -1, jnp.int32)
        for j in range(full):
            ids[a, pl.ds(j, 1), :] = tet_ref[pl.ds(a, 1), pl.ds(j * LANES, LANES)]
        rest = elems - full * LANES
        if rest:
            ids[a, pl.ds(full, 1), pl.ds(0, rest)] = tet_ref[pl.ds(a, 1), pl.ds(full * LANES, rest)]

    def build(q, carry):
        lane = lax.broadcasted_iota(jnp.int32, (LANES, LANES), 0)
        for a in range(4):
            low = jnp.broadcast_to(ids[a, pl.ds(q, 1), :] & (LANES - 1), (LANES, LANES))
            hot = jnp.where(low == lane, 1.0, 0.0).astype(BF16)
            onehot[:, pl.ds(pl.multiple_of((q * 4 + a) * LANES, LANES), LANES)] = hot
        return carry

    lax.fori_loop(0, tet_rows, build, 0)

    def node_sums():
        def spread_rows(q, carry):
            level = lax.broadcasted_iota(jnp.int32, (8, LANES), 0) + 2
            for a in range(4):
                high = jnp.broadcast_to(ids[a, pl.ds(q, 1), :] >> 7, (8, LANES))
                val = jnp.broadcast_to(vals[a, pl.ds(q, 1), :], (8, LANES))
                one, two, three = pieces(jnp.where(high == level, val, 0.0))
                block = jnp.concatenate([one, two, three, jnp.zeros((8, LANES), F32)], axis=0)
                spread[:, pl.ds(pl.multiple_of((q * 4 + a) * LANES, LANES), LANES)] = block.astype(BF16)
            return carry

        lax.fori_loop(0, tet_rows, spread_rows, 0)

        def accumulate(i, total):
            at = pl.ds(pl.multiple_of(i * CHUNK, CHUNK), CHUNK)
            return total + lax.dot_general(
                spread[:, at], onehot[:, at], (((1,), (1,)), ((), ())), preferred_element_type=F32)

        total = lax.fori_loop(0, onehot.shape[1] // CHUNK, accumulate, jnp.zeros((32, LANES), F32))
        return total[0:8] + total[8:16] + total[16:24]

    finish(coords_sent)
    finish(static_sent)
    static_sent = gather_stage(g_ref, 0, 1)

    def shape_elements(i, carry):
        at = pl.ds(pl.multiple_of(i * 8, 8), 8)
        corner = [ids[a, at, :] for a in range(4)]
        spots = []
        for a in range(4):
            low, high = corner[a] & (LANES - 1), corner[a] >> 7
            xyz = [jnp.zeros((8, LANES), F32) for _ in range(3)]
            for r in range(12):
                hit = high == r
                for k in range(3):
                    line = jnp.broadcast_to(ext_c[r, pl.ds(k, 1), :], (8, LANES))
                    xyz[k] = jnp.where(hit, lane_pick(line, low), xyz[k])
            spots.append(xyz)
        edges = [[spots[a][k] - spots[0][k] for k in range(3)] for a in range(1, 4)]
        n1 = cross(edges[1], edges[2])
        n2 = cross(edges[2], edges[0])
        n3 = cross(edges[0], edges[1])
        n0 = tuple(-(n1[k] + n2[k] + n3[k]) for k in range(3))
        present = corner[0] >= 0
        volume = jnp.abs(jnp.where(present, dot3(edges[0], n1), 1.0))
        weight = jnp.where(present, 1.0 / (6.0 * volume), 0.0)
        normals = (n0, n1, n2, n3)
        for e, (a, b) in enumerate(PAIRS):
            value = dot3(normals[a], normals[b]) * weight
            stiff[e, at, :] = value
            if a == b:
                vals[a, at, :] = value
        return carry

    lax.fori_loop(0, tet_rows // 8, shape_elements, 0)
    reaction = rea_ref[...]
    diagonal = reaction + node_sums()
    finish(static_sent)
    static_sent = gather_stage(g_ref, 0, 2)

    resid = load_ref[...]
    x = direction = image = gamma_old = alpha = None
    for k in range(ITERS):
        table = ext_v.at[k]
        precond = resid / diagonal
        for s in range(8):
            table[2 + s] = jnp.broadcast_to(precond[s : s + 1, :], (8, LANES))
        finish(halo(table, 1 + k))

        def products(i, carry):
            at = pl.ds(pl.multiple_of(i * 8, 8), 8)
            corner = []
            for a in range(4):
                corner.append(pick([table[r] for r in range(12)], ids[a, at, :]))
            sums = [None] * 4
            for e, (a, b) in enumerate(PAIRS):
                value = stiff[e, at, :]
                for m, n in {(a, b), (b, a)}:
                    term = value * corner[n]
                    sums[m] = term if sums[m] is None else sums[m] + term
            for a in range(4):
                vals[a, at, :] = sums[a]
            return carry

        lax.fori_loop(0, tet_rows // 8, products, 0)
        applied = reaction * precond + node_sums()
        gamma, delta = reduce_all(resid * precond, precond * applied, k)
        if k == 0:
            alpha = gamma / delta
            direction, image = precond, applied
            x = alpha * direction
        else:
            beta = gamma / gamma_old
            alpha = gamma / (delta - beta * gamma / alpha)
            direction = precond + beta * direction
            image = applied + beta * image
            x = x + alpha * direction
        if k + 1 < ITERS:
            resid = resid - alpha * image
        gamma_old = gamma

    sol_ref[...] = x
    tables = [jnp.broadcast_to(x[s : s + 1, :], (8, LANES)) for s in range(8)]
    t_ref[z_hi, y, z_lo, g] = pick(tables, slot_ids)
    finish(static_sent)
    for stage in range(3):
        finish(gather_stage(t_ref, 1, stage))


def pair_kernel(g_ref, t_ref, out_ref, lhs, acc, rows):
    row, col = lax.axis_index("row"), lax.axis_index("col")
    me = row * 16 + col
    count = out_ref.shape[1]
    padded = acc.shape[0]

    def trace_row(p):
        tile = t_ref[p]
        return jnp.concatenate([tile[j : j + 1, :] for j in range(SLOTS // LANES)], axis=1)

    own = g_ref[me]
    first = jnp.max(jnp.where(own[6:7] > 0, 1.0, 0.0) * own[0:3] + jnp.where(own[6:7] > 0, 0.0, -1e9), axis=1, keepdims=True)
    centre = jnp.concatenate([first, jnp.zeros((5, 1), F32)], axis=0)
    t = own[0:3] - first
    t_one, t_two, t_three = pieces(t)
    q_one, q_two, q_three = pieces(dot3((t[0:1], t[1:2], t[2:3]), (t[0:1], t[1:2], t[2:3])))
    none3 = jnp.zeros((3, SLOTS), F32)
    none1 = jnp.zeros((1, SLOTS), F32)
    unit = jnp.ones((1, SLOTS), F32)
    blocks_d, blocks_n = [], []
    for part, lead in ((t_one, 1), (t_two, 0), (t_three, 0), (t_one, 1), (t_two, 0), (t_one, 1)):
        flag = unit if lead else none1
        blocks_d += [-2.0 * part, none3, flag, none1]
        blocks_n += [none3, part, none1, -flag]
    blocks_d += [q_one, q_two, q_three] + [none1] * 13
    blocks_n += [none1] * 16
    fill = jnp.zeros((64, SLOTS), F32)
    for i, blocks in enumerate((blocks_d, blocks_n)):
        stacked = jnp.concatenate(blocks + [fill], axis=0)
        lhs[i] = stacked.T[0:padded, 0:64].astype(BF16)
    acc[...] = jnp.zeros_like(acc)
    rows[...] = jnp.zeros_like(rows)
    rows[pl.ds(48, 8), :] = jnp.where(lax.broadcasted_iota(jnp.int32, (8, SLOTS), 0) < 3, 1.0, 0.0).astype(F32)

    def step(p, carry):
        tile = g_ref[p]
        trace = trace_row(p)
        s = tile[0:3] - first
        w = tile[3:6] * trace
        sx, wx = [s[k : k + 1] for k in range(3)], [w[k : k + 1] for k in range(3)]
        data = jnp.concatenate([s, w, dot3(sx, sx) + 0.25, dot3(sx, wx)], axis=0)
        one, two, three = pieces(data)
        for i, part in enumerate((one, one, one, two, two, three)):
            rows[pl.ds(8 * i, 8), :] = part
        rhs = rows[...].astype(BF16)
        for m in range(0, padded, 64):
            d = jnp.dot(lhs[0, m : m + 64, :], rhs, preferred_element_type=F32)
            n = jnp.dot(lhs[1, m : m + 64, :], rhs, preferred_element_type=F32)
            inv = lax.rsqrt(d)
            c = (n * inv) * (inv * inv)
            acc[m : m + 64, :] += (c[:, 0:128] + c[:, 128:256]) + (c[:, 256:384] + c[:, 384:512])
        return carry

    lax.fori_loop(0, g_ref.shape[0], step, 0)
    sums = jnp.sum(acc[...].T, axis=0, keepdims=True) * (0.25 / math.pi)
    trace = trace_row(me)
    result = own[6:7, 0:padded] * (-0.5 * trace[:, 0:padded] + sums)
    out_ref[...] = result[:, 0:count]


def local(node_coords, tet_nodes, bnd_nodes, reaction, load, area_normal):
    elems, count = tet_nodes.shape[1], bnd_nodes.shape[0]
    tet_rows = -(-elems // 1024) * 8
    length = 4 * tet_rows * LANES
    sol, gathered, traces = pl.pallas_call(
        chain_kernel,
        out_shape=(
            jax.ShapeDtypeStruct((8, LANES), F32),
            jax.ShapeDtypeStruct((2, 4, 2, 8, 8, SLOTS), F32),
            jax.ShapeDtypeStruct((2, 4, 2, 8, 8, LANES), F32),
        ),
        in_specs=[VMEM] * 6,
        out_specs=(VMEM,) * 3,
        scratch_shapes=[
            pltpu.VMEM((4, tet_rows, LANES), jnp.int32),
            pltpu.VMEM((12, 8, LANES), F32),
            pltpu.VMEM((ITERS, 12, 8, LANES), F32),
            pltpu.VMEM((LANES, length), BF16),
            pltpu.VMEM((32, length), BF16),
            pltpu.VMEM((10, tet_rows, LANES), F32),
            pltpu.VMEM((4, tet_rows, LANES), F32),
            pltpu.VMEM((8, LANES), jnp.int32),
            pltpu.VMEM((ITERS, 8, 2, 8, LANES), F32),
            pltpu.VMEM((ITERS, 4, 2, 8, LANES), F32),
            pltpu.VMEM((ITERS, 4, 2, 8, LANES), F32),
            pltpu.SemaphoreType.DMA((1 + ITERS, 2)),
            pltpu.SemaphoreType.DMA((1 + ITERS, 2)),
            pltpu.SemaphoreType.DMA((ITERS, 13)),
            pltpu.SemaphoreType.DMA((ITERS, 13)),
            pltpu.SemaphoreType.DMA((2, 13)),
            pltpu.SemaphoreType.DMA((2, 13)),
        ],
        compiler_params=pltpu.CompilerParams(collective_id=0, has_side_effects=True, vmem_limit_bytes=60 << 20),
        name="chain",
    )(tet_nodes, node_coords, bnd_nodes.reshape(1, count), area_normal,
      reaction.reshape(8, LANES), load.reshape(8, LANES))
    padded = -(-count // 64) * 64
    demag = pl.pallas_call(
        pair_kernel,
        out_shape=jax.ShapeDtypeStruct((1, count), F32),
        in_specs=[VMEM] * 2,
        out_specs=VMEM,
        scratch_shapes=[
            pltpu.VMEM((2, padded, 64), BF16),
            pltpu.VMEM((padded, LANES), F32),
            pltpu.VMEM((64, SLOTS), F32),
        ],
        compiler_params=pltpu.CompilerParams(vmem_limit_bytes=60 << 20),
        name="pairs",
    )(gathered.reshape(128, 8, SLOTS), traces.reshape(128, 8, LANES))
    return sol.reshape(-1), demag.reshape(-1)


def solution(mesh):
    placed = (
        P(None, ("row", "col")),
        P(None, ("row", "col")),
        P(("row", "col")),
        P(("row", "col")),
        P(("row", "col")),
        P(None, ("row", "col")),
    )
    return jax.shard_map(
        local,
        mesh=mesh,
        in_specs=placed,
        out_specs=(P(("row", "col")), P(("row", "col"))),
        check_vma=False,
    )
```

```python
import functools
import math

import jax
import jax.numpy as jnp
from jax import lax
from jax.experimental import pallas as pl
from jax.experimental.pallas import tpu as pltpu
from jax.sharding import PartitionSpec as P

ITERS = 3
LANES = 128
SLOTS = 512
F32 = jnp.float32
BF16 = jnp.bfloat16
MESH = pl.DeviceIdType.MESH
VMEM = pl.BlockSpec(memory_space=pltpu.VMEM)
CHUNK = 2048
QS = 16
WIDE = 256
MAIN = 4 * 4 * (QS - 1)
BLOCK = 240
UNROLL = 6
PAIRS = [(a, b) for a in range(4) for b in range(a, 4)]


def place():
    row, col = lax.axis_index("row"), lax.axis_index("col")
    z_hi, y = row // 4, row % 4
    z_lo, g = col // 8, col % 8
    return row, col, z_hi, y, z_lo, g


def peers():
    row, col, z_hi, y, z_lo, g = place()
    out = [(row, z_lo * 8 + (g + j) % 8) for j in range(1, 8)]
    out += [(z_hi * 4 + (y + j) % 4, col) for j in range(1, 4)]
    z = z_hi * 2 + z_lo
    for j in range(1, 4):
        other = (z + j) % 4
        out.append(((other // 2) * 4 + y, (other % 2) * 8 + g))
    return out


def lane_pick(table, low):
    return jnp.take_along_axis(table, low, axis=1, mode="promise_in_bounds")


def pick(rows, ids):
    low = ids & (LANES - 1)
    high = ids >> 7
    out = jnp.zeros(ids.shape, F32)
    for r, row in enumerate(rows):
        out = jnp.where(high == r, lane_pick(row, low), out)
    return out


def pieces(v):
    one = v.astype(BF16).astype(F32)
    rest = v - one
    two = rest.astype(BF16).astype(F32)
    return one, two, rest - two


def cross(u, v):
    return (
        u[1] * v[2] - u[2] * v[1],
        u[2] * v[0] - u[0] * v[2],
        u[0] * v[1] - u[1] * v[0],
    )


def dot3(u, v):
    return u[0] * v[0] + u[1] * v[1] + u[2] * v[2]


def full_kernel(
    tet_ref, nc_ref, bnd_ref, an_ref, rea_ref, load_ref,
    sol_ref, out_ref,
    ids, ext_c, ext_v, onehot, spread, stiff, vals, slots, chosen, order,
    source, trace, near, far, rhs, lhs, part, fin, fex,
    red_a, red_y, red_z,
    halo_s, halo_r, red_s, red_r, all_s, all_r, near_s, near_r, far_s, far_r,
    fin_s, fin_r, fex_s, fex_r,
):
    row, col, z_hi, y, z_lo, g = place()
    z = z_hi * 2 + z_lo
    others = peers()
    before, after = (row, (col + 15) % 16), (row, (col + 1) % 16)
    partner = (row, (1 - z_lo) * 8 + g)
    column = [((row + j) % 8, col) for j in range(1, 8)]
    keeper = (col % 8, (1 - col // 8) * 15)
    at_end = col % 15 == 0
    helped = row + (1 - col // 15) * 8
    helpers = [(r, helped) for r in range(8)]
    elems = tet_ref.shape[1]
    count = bnd_ref.shape[1]
    tet_rows = ids.shape[1]

    fex[...] = jnp.zeros(fex.shape, F32)
    part[...] = jnp.zeros(part.shape, F32)

    barrier = pltpu.get_barrier_semaphore()
    greeted = others + column + [before, after, keeper]
    for who in greeted:
        pl.semaphore_signal(barrier, inc=1, device_id=who, device_id_type=MESH)

    @pl.when(at_end)
    def _():
        for who in helpers:
            pl.semaphore_signal(barrier, inc=1, device_id=who, device_id_type=MESH)

    def remote(src, dst, ssem, rsem, who):
        return pltpu.make_async_remote_copy(
            src_ref=src, dst_ref=dst, send_sem=ssem, recv_sem=rsem,
            device_id=who, device_id_type=MESH,
        )

    def send(*args):
        copy = remote(*args)
        copy.start()
        return copy

    def halo(buf, k):
        return [
            send(buf.at[pl.ds(2, 2)], buf.at[pl.ds(10, 2)], halo_s.at[k, 0], halo_r.at[k, 0], before),
            send(buf.at[pl.ds(8, 2)], buf.at[pl.ds(0, 2)], halo_s.at[k, 1], halo_r.at[k, 1], after),
        ]

    def share(buf, k):
        tile = buf.at[col]
        return [send(tile, tile, all_s.at[k, j], all_r.at[k, j], others[j]) for j in range(7)]

    def share_on(buf, k):
        tiles = buf.at[pl.ds(z_lo * 8, 8)]
        return [send(tiles, tiles, all_s.at[k, 7], all_r.at[k, 7], partner)]

    def finish(copies):
        for copy in copies:
            copy.wait()

    def reduce_all(u, v, k):
        for buf, mine, size, first in ((red_a, g, 8, 0), (red_y, y, 4, 7), (red_z, z, 4, 10)):
            here = buf.at[k]
            here[mine, 0] = u
            here[mine, 1] = v
            tile = here.at[mine]
            finish([
                send(tile, tile, red_s.at[k, first + j], red_r.at[k, first + j], others[first + j])
                for j in range(size - 1)
            ])
            u, v = here[0, 0], here[0, 1]
            for i in range(1, size):
                u, v = u + here[i, 0], v + here[i, 1]
        return jnp.sum(u, keepdims=True), jnp.sum(v, keepdims=True)

    for s in range(8):
        for k in range(3):
            ext_c[2 + s, pl.ds(k, 1), :] = nc_ref[pl.ds(k, 1), pl.ds(s * LANES, LANES)]
        ext_c[2 + s, pl.ds(3, 5), :] = jnp.zeros((5, LANES), F32)

    slots[...] = jnp.full(slots.shape, -1, jnp.int32)
    for j in range(SLOTS // LANES):
        width = min(LANES, count - j * LANES)
        slots[pl.ds(j, 1), pl.ds(0, width)] = bnd_ref[:, pl.ds(j * LANES, width)]
    slot_ids = slots[...]
    live = jnp.where(slot_ids >= 0, 1.0, 0.0)
    tri = lax.broadcasted_iota(jnp.int32, (LANES, LANES), 0) <= lax.broadcasted_iota(jnp.int32, (LANES, LANES), 1)
    tri = jnp.where(tri, 1.0, 0.0).astype(BF16)
    rank = jnp.dot(live.astype(BF16), tri, preferred_element_type=F32) - 1.0
    totals = jnp.sum(live, axis=1, keepdims=True)
    base = jnp.zeros((1, 1), F32)
    bases = []
    for j in range(8):
        bases.append(base)
        base = base + totals[j : j + 1]
    rank = rank + jnp.concatenate(bases, axis=0)
    spot = (rank + jnp.where(rank >= MAIN, 1.0 * (WIDE - MAIN), 0.0)).astype(jnp.int32)
    spot = jnp.where(slot_ids >= 0, spot, -1)
    for j in range(SLOTS // LANES):
        line = jnp.broadcast_to(spot[j : j + 1, :], (SLOTS, LANES))
        hot = jnp.where(line == lax.broadcasted_iota(jnp.int32, (SLOTS, LANES), 0), 1.0, 0.0)
        order[:, pl.ds(j * LANES, LANES)] = hot.astype(BF16)
    tile = source.at[col]
    tile[...] = jnp.zeros((8, SLOTS), F32)
    for j in range(SLOTS // LANES):
        tile[pl.ds(0, 1), pl.ds(j * LANES, LANES)] = (slot_ids[j : j + 1, :] + 1).astype(F32)
    for k in range(3):
        tile[pl.ds(1 + k, 1), pl.ds(0, count)] = an_ref[pl.ds(k, 1), :]
    one, two, three = pieces(tile[...])
    stacked = jnp.concatenate([one, two, three, jnp.zeros((8, SLOTS), F32)], axis=0).astype(BF16)
    moved = lax.dot_general(stacked, order[...], (((1,), (1,)), ((), ())), preferred_element_type=F32)
    moved = moved[0:8] + moved[8:16] + moved[16:24]
    chosen[...] = jnp.full(chosen.shape, -1, jnp.int32)
    for j in range(SLOTS // LANES):
        chosen[pl.ds(j, 1), :] = moved[0:1, j * LANES : (j + 1) * LANES].astype(jnp.int32) - 1
    nodes = chosen[...]
    tile[pl.ds(3, 3), :] = moved[1:4]
    for k in range(3):
        tables = [jnp.broadcast_to(ext_c[2 + s, pl.ds(k, 1), :], (8, LANES)) for s in range(8)]
        where = pick(tables, nodes)
        for j in range(SLOTS // LANES):
            tile[pl.ds(k, 1), pl.ds(j * LANES, LANES)] = where[j : j + 1, :]
    near[row] = tile[:, 0:WIDE]

    pl.semaphore_wait(barrier, len(greeted) + 8 * at_end.astype(jnp.int32))
    coords_sent = halo(ext_c, 0)
    static_sent = share(source, 0)
    mine = near.at[row]
    column_sent = [send(mine, mine, near_s.at[j], near_r.at[j], column[j]) for j in range(7)]

    @pl.when(at_end)
    def _():
        for r in range(8):
            remote(tile.at[:, pl.ds(WIDE, WIDE)], far, far_s.at[r], far_r, helpers[r]).start()

    full = elems // LANES
    for a in range(4):
        ids[a, pl.ds(full // 8 * 8, tet_rows - full // 8 * 8), :] = jnp.full(
            (tet_rows - full // 8 * 8, LANES), -1, jnp.int32)
        for j in range(full):
            ids[a, pl.ds(j, 1), :] = tet_ref[pl.ds(a, 1), pl.ds(j * LANES, LANES)]
        rest = elems - full * LANES
        if rest:
            ids[a, pl.ds(full, 1), pl.ds(0, rest)] = tet_ref[pl.ds(a, 1), pl.ds(full * LANES, rest)]

    def build(q, carry):
        lane = lax.broadcasted_iota(jnp.int32, (LANES, LANES), 0)
        for a in range(4):
            low = jnp.broadcast_to(ids[a, pl.ds(q, 1), :] & (LANES - 1), (LANES, LANES))
            hot = jnp.where(low == lane, 1.0, 0.0).astype(BF16)
            onehot[:, pl.ds(pl.multiple_of((q * 4 + a) * LANES, LANES), LANES)] = hot
        return carry

    lax.fori_loop(0, tet_rows, build, 0)

    def node_sums():
        def spread_rows(q, carry):
            level = lax.broadcasted_iota(jnp.int32, (8, LANES), 0) + 2
            for a in range(4):
                high = jnp.broadcast_to(ids[a, pl.ds(q, 1), :] >> 7, (8, LANES))
                val = jnp.broadcast_to(vals[a, pl.ds(q, 1), :], (8, LANES))
                one, two, three = pieces(jnp.where(high == level, val, 0.0))
                block = jnp.concatenate([one, two, three, jnp.zeros((8, LANES), F32)], axis=0)
                spread[:, pl.ds(pl.multiple_of((q * 4 + a) * LANES, LANES), LANES)] = block.astype(BF16)
            return carry

        lax.fori_loop(0, tet_rows, spread_rows, 0)

        def accumulate(i, total):
            at = pl.ds(pl.multiple_of(i * CHUNK, CHUNK), CHUNK)
            return total + lax.dot_general(
                spread[:, at], onehot[:, at], (((1,), (1,)), ((), ())), preferred_element_type=F32)

        total = lax.fori_loop(0, onehot.shape[1] // CHUNK, accumulate, jnp.zeros((32, LANES), F32))
        return total[0:8] + total[8:16] + total[16:24]

    finish(coords_sent)

    def shape_elements(i, carry):
        at = pl.ds(pl.multiple_of(i * 8, 8), 8)
        corner = [ids[a, at, :] for a in range(4)]
        spots = []
        for a in range(4):
            low, high = corner[a] & (LANES - 1), corner[a] >> 7
            xyz = [jnp.zeros((8, LANES), F32) for _ in range(3)]
            for r in range(12):
                hit = high == r
                for k in range(3):
                    line = jnp.broadcast_to(ext_c[r, pl.ds(k, 1), :], (8, LANES))
                    xyz[k] = jnp.where(hit, lane_pick(line, low), xyz[k])
            spots.append(xyz)
        edges = [[spots[a][k] - spots[0][k] for k in range(3)] for a in range(1, 4)]
        n1 = cross(edges[1], edges[2])
        n2 = cross(edges[2], edges[0])
        n3 = cross(edges[0], edges[1])
        n0 = tuple(-(n1[k] + n2[k] + n3[k]) for k in range(3))
        present = corner[0] >= 0
        volume = jnp.abs(jnp.where(present, dot3(edges[0], n1), 1.0))
        weight = jnp.where(present, 1.0 / (6.0 * volume), 0.0)
        normals = (n0, n1, n2, n3)
        for e, (a, b) in enumerate(PAIRS):
            value = dot3(normals[a], normals[b]) * weight
            stiff[e, at, :] = value
            if a == b:
                vals[a, at, :] = value
        return carry

    lax.fori_loop(0, tet_rows // 8, shape_elements, 0)
    finish(static_sent)
    static_sent = share_on(source, 0)
    reaction = rea_ref[...]
    diagonal = reaction + node_sums()

    resid = load_ref[...]
    x = direction = image = gamma_old = alpha = None
    for k in range(ITERS):
        table = ext_v.at[k]
        precond = resid / diagonal
        for s in range(8):
            table[2 + s] = jnp.broadcast_to(precond[s : s + 1, :], (8, LANES))
        finish(halo(table, 1 + k))

        def products(i, carry):
            at = pl.ds(pl.multiple_of(i * 8, 8), 8)
            corner = []
            for a in range(4):
                corner.append(pick([table[r] for r in range(12)], ids[a, at, :]))
            sums = [None] * 4
            for e, (a, b) in enumerate(PAIRS):
                value = stiff[e, at, :]
                for m, n in {(a, b), (b, a)}:
                    term = value * corner[n]
                    sums[m] = term if sums[m] is None else sums[m] + term
            for a in range(4):
                vals[a, at, :] = sums[a]
            return carry

        lax.fori_loop(0, tet_rows // 8, products, 0)
        applied = reaction * precond + node_sums()
        gamma, delta = reduce_all(resid * precond, precond * applied, k)
        if k == 0:
            alpha = gamma / delta
            direction, image = precond, applied
            x = alpha * direction
        else:
            beta = gamma / gamma_old
            alpha = gamma / (delta - beta * gamma / alpha)
            direction = precond + beta * direction
            image = applied + beta * image
            x = x + alpha * direction
        if k + 1 < ITERS:
            resid = resid - alpha * image
        gamma_old = gamma

    sol_ref[...] = x
    tables = [jnp.broadcast_to(x[s : s + 1, :], (8, LANES)) for s in range(8)]
    trace[col] = pick(tables, nodes)
    trace_sent = share(trace, 1)
    own_trace = pick(tables, slot_ids)

    def split_target(b, tile, first):
        t = tile[0:3] - first
        t_one, t_two, t_three = pieces(t)
        q_one, q_two, q_three = pieces(dot3((t[0:1], t[1:2], t[2:3]), (t[0:1], t[1:2], t[2:3])))
        none3, none1 = jnp.zeros((3, WIDE), F32), jnp.zeros((1, WIDE), F32)
        unit = jnp.ones((1, WIDE), F32)
        blocks_d, blocks_n = [], []
        for piece, lead in ((t_one, 1), (t_two, 0), (t_three, 0), (t_one, 1), (t_two, 0), (t_one, 1)):
            flag = unit if lead else none1
            blocks_d += [-2.0 * piece, none3, flag, none1]
            blocks_n += [none3, piece, none1, -flag]
        blocks_d += [q_one, q_two, q_three] + [none1] * 13
        blocks_n += [none1] * 16
        fill = jnp.zeros((64, WIDE), F32)
        for i, blocks in enumerate((blocks_d, blocks_n)):
            lhs[b, i] = jnp.concatenate(blocks + [fill], axis=0).T[:, 0:64].astype(BF16)

    finish(static_sent)
    finish(column_sent)
    remote(far, far, far_s.at[0], far_r, keeper).wait_recv()

    @pl.when(at_end)
    def _():
        for r in range(8):
            remote(tile.at[:, pl.ds(WIDE, WIDE)], far, far_s.at[r], far_r, helpers[r]).wait_send()

    own_first = near[row][0:3, 0:1]
    far_first = far[0:3, 0:1]

    def split_near(b, carry):
        split_target(b, near[b], own_first)
        return carry

    lax.fori_loop(0, 8, split_near, 0)
    split_target(8, far[...], far_first)

    finish(trace_sent)
    finish(share_on(trace, 1))

    def split_sources(first):
        unit = jnp.where(lax.broadcasted_iota(jnp.int32, (8, WIDE), 0) < 3, 1.0, 0.0).astype(F32)

        def put(i, tile, tr):
            s = tile[0:3] - first
            w = tile[3:6] * tr
            sx, wx = [s[k : k + 1] for k in range(3)], [w[k : k + 1] for k in range(3)]
            data = jnp.concatenate([s, w, dot3(sx, sx) + 0.25, dot3(sx, wx)], axis=0)
            one, two, three = pieces(data)
            block = jnp.concatenate([one, one, one, two, two, three, unit, jnp.zeros((8, WIDE), F32)], axis=0)
            rhs[:, pl.ds(pl.multiple_of(i * WIDE, WIDE), WIDE)] = block.astype(BF16)

        def each(c, carry):
            tr = trace[c]
            put(c, source[c, :, pl.ds(0, WIDE)], jnp.concatenate([tr[0:1], tr[1:2]], axis=1))
            return carry

        lax.fori_loop(0, 16, each, 0)
        for i, c in ((16, 0), (17, 15)):
            tr = trace[c]
            put(i, source[c, :, pl.ds(WIDE, WIDE)], jnp.concatenate([tr[2:3], tr[3:4]], axis=1))

    def pair_sums(b):
        parts = []
        for low, high in ((0, 128), (128, BLOCK)):
            left_d, left_n = lhs[b, 0, low:high, :], lhs[b, 1, low:high, :]

            def some(i, total):
                for u in range(UNROLL):
                    right = rhs[:, pl.ds(pl.multiple_of((i * UNROLL + u) * WIDE, WIDE), WIDE)]
                    d = jnp.dot(left_d, right, preferred_element_type=F32)
                    n = jnp.dot(left_n, right, preferred_element_type=F32)
                    inv = lax.rsqrt(d)
                    c = (n * inv) * (inv * inv)
                    total = total + (c[:, 0:LANES] + c[:, LANES:WIDE])
                return total

            parts.append(lax.fori_loop(0, 18 // UNROLL, some, jnp.zeros((high - low, LANES), F32)))
        parts.append(jnp.zeros((WIDE - BLOCK, LANES), F32))
        return jnp.sum(jnp.concatenate(parts, axis=0).T, axis=0, keepdims=True)

    def keep(ref, sums):
        ref[pl.ds(0, 1), :] = sums[:, 0:LANES]
        ref[pl.ds(1, 1), :] = sums[:, LANES:WIDE]

    split_sources(far_first)
    keep(part.at[8], pair_sums(8))
    fex_sent = send(part.at[8], fex.at[row], fex_s, fex_r.at[row], keeper)
    split_sources(own_first)

    def one_row(j, carry):
        other = (row + j) % 8
        keep(part.at[other], pair_sums(other))
        remote(part.at[other], fin.at[row], fin_s.at[j - 1], fin_r.at[j - 1], (other, col)).start()
        return carry

    lax.fori_loop(1, 8, one_row, 0)
    keep(part.at[row], pair_sums(row))
    fin[row] = part[row]
    fex_sent.wait_send()
    for j in range(7):
        remote(part.at[row], fin.at[row], fin_s.at[j], fin_r.at[j], column[j]).wait()

    @pl.when(at_end)
    def _():
        for r in range(8):
            remote(part.at[8], fex.at[r], fex_s, fex_r.at[r], keeper).wait_recv()

    total, more = fin[0], fex[0]
    for r in range(1, 8):
        total, more = total + fin[r], more + fex[r]
    tables = [jnp.broadcast_to(v[j : j + 1, :], (8, LANES)) for v in (total, more) for j in range(2)]
    result = live * (-0.5 * own_trace + (0.25 / math.pi) * pick(tables, spot))
    for j in range(SLOTS // LANES):
        width = min(LANES, count - j * LANES)
        out_ref[:, pl.ds(j * LANES, width)] = result[j : j + 1, 0:width]


def local(node_coords, tet_nodes, bnd_nodes, reaction, load, area_normal):
    elems, count = tet_nodes.shape[1], bnd_nodes.shape[0]
    tet_rows = -(-elems // 1024) * 8
    length = 4 * tet_rows * LANES
    dma = pltpu.SemaphoreType.DMA
    sol, demag = pl.pallas_call(
        full_kernel,
        out_shape=(
            jax.ShapeDtypeStruct((8, LANES), F32),
            jax.ShapeDtypeStruct((1, count), F32),
        ),
        in_specs=[VMEM] * 6,
        out_specs=(VMEM,) * 2,
        scratch_shapes=[
            pltpu.VMEM((4, tet_rows, LANES), jnp.int32),
            pltpu.VMEM((12, 8, LANES), F32),
            pltpu.VMEM((ITERS, 12, 8, LANES), F32),
            pltpu.VMEM((LANES, length), BF16),
            pltpu.VMEM((32, length), BF16),
            pltpu.VMEM((10, tet_rows, LANES), F32),
            pltpu.VMEM((4, tet_rows, LANES), F32),
            pltpu.VMEM((8, LANES), jnp.int32),
            pltpu.VMEM((8, LANES), jnp.int32),
            pltpu.VMEM((SLOTS, SLOTS), BF16),
            pltpu.VMEM((16, 8, SLOTS), F32),
            pltpu.VMEM((16, 8, LANES), F32),
            pltpu.VMEM((8, 8, WIDE), F32),
            pltpu.VMEM((8, WIDE), F32),
            pltpu.VMEM((64, 18 * WIDE), BF16),
            pltpu.VMEM((9, 2, WIDE, 64), BF16),
            pltpu.VMEM((9, 8, LANES), F32),
            pltpu.VMEM((8, 8, LANES), F32),
            pltpu.VMEM((8, 8, LANES), F32),
            pltpu.VMEM((ITERS, 8, 2, 8, LANES), F32),
            pltpu.VMEM((ITERS, 4, 2, 8, LANES), F32),
            pltpu.VMEM((ITERS, 4, 2, 8, LANES), F32),
            dma((1 + ITERS, 2)), dma((1 + ITERS, 2)),
            dma((ITERS, 13)), dma((ITERS, 13)),
            dma((2, 8)), dma((2, 8)),
            dma((7,)), dma((7,)),
            dma((8,)), dma(()),
            dma((7,)), dma((7,)),
            dma(()), dma((8,)),
        ],
        compiler_params=pltpu.CompilerParams(collective_id=0, has_side_effects=True, vmem_limit_bytes=60 << 20),
        name="full",
    )(tet_nodes, node_coords, bnd_nodes.reshape(1, count), area_normal,
      reaction.reshape(8, LANES), load.reshape(8, LANES))
    return sol.reshape(-1), demag.reshape(-1)


def solution(mesh):
    placed = (
        P(None, ("row", "col")),
        P(None, ("row", "col")),
        P(("row", "col")),
        P(("row", "col")),
        P(("row", "col")),
        P(None, ("row", "col")),
    )
    return jax.shard_map(
        local,
        mesh=mesh,
        in_specs=placed,
        out_specs=(P(("row", "col")), P(("row", "col"))),
        check_vma=False,
    )
```

```python
import functools
import math

import jax
import jax.numpy as jnp
from jax import lax
from jax.experimental import pallas as pl
from jax.experimental.pallas import tpu as pltpu
from jax.sharding import PartitionSpec as P

ITERS = 3
LANES = 128
SLOTS = 512
F32 = jnp.float32
BF16 = jnp.bfloat16
MESH = pl.DeviceIdType.MESH
VMEM = pl.BlockSpec(memory_space=pltpu.VMEM)
CHUNK = 7168
QS = 16
WIDE = 256
MAIN = 4 * 4 * (QS - 1)
BLOCK = 240
UNROLL = 6
PAIRS = [(a, b) for a in range(4) for b in range(a, 4)]


def place():
    row, col = lax.axis_index("row"), lax.axis_index("col")
    z_hi, y = row // 4, row % 4
    z_lo, g = col // 8, col % 8
    return row, col, z_hi, y, z_lo, g


def peers():
    row, col, z_hi, y, z_lo, g = place()
    out = [(row, z_lo * 8 + (g + j) % 8) for j in range(1, 8)]
    out += [(z_hi * 4 + (y + j) % 4, col) for j in range(1, 4)]
    z = z_hi * 2 + z_lo
    for j in range(1, 4):
        other = (z + j) % 4
        out.append(((other // 2) * 4 + y, (other % 2) * 8 + g))
    return out


def lane_pick(table, low):
    return jnp.take_along_axis(table, low, axis=1, mode="promise_in_bounds")


def pick(rows, ids):
    low = ids & (LANES - 1)
    high = ids >> 7
    out = jnp.zeros(ids.shape, F32)
    for r, row in enumerate(rows):
        out = jnp.where(high == r, lane_pick(row, low), out)
    return out


def pieces(v):
    one = v.astype(BF16).astype(F32)
    rest = v - one
    two = rest.astype(BF16).astype(F32)
    return one, two, rest - two


def cross(u, v):
    return (
        u[1] * v[2] - u[2] * v[1],
        u[2] * v[0] - u[0] * v[2],
        u[0] * v[1] - u[1] * v[0],
    )


def dot3(u, v):
    return u[0] * v[0] + u[1] * v[1] + u[2] * v[2]


def full_kernel(
    tet_ref, nc_ref, bnd_ref, an_ref, rea_ref, load_ref,
    sol_ref, out_ref,
    ids, ext_c, ext_v, onehot, spread, stiff, vals, slots, chosen, order,
    source, trace, near, far, rhs, lhs, part, fin, fex,
    red_a, red_y, red_z,
    halo_s, halo_r, red_s, red_r, all_s, all_r, near_s, near_r, far_s, far_r,
    fin_s, fin_r, fex_s, fex_r,
):
    row, col, z_hi, y, z_lo, g = place()
    z = z_hi * 2 + z_lo
    others = peers()
    before, after = (row, (col + 15) % 16), (row, (col + 1) % 16)
    partner = (row, (1 - z_lo) * 8 + g)
    column = [((row + j) % 8, col) for j in range(1, 8)]
    keeper = (col % 8, (1 - col // 8) * 15)
    at_end = col % 15 == 0
    helped = row + (1 - col // 15) * 8
    helpers = [(r, helped) for r in range(8)]
    elems = tet_ref.shape[1]
    count = bnd_ref.shape[1]
    tet_rows = ids.shape[1]

    fex[...] = jnp.zeros(fex.shape, F32)
    part[...] = jnp.zeros(part.shape, F32)

    barrier = pltpu.get_barrier_semaphore()
    greeted = others + [before, after]
    for who in greeted:
        pl.semaphore_signal(barrier, inc=1, device_id=who, device_id_type=MESH)

    def remote(src, dst, ssem, rsem, who):
        return pltpu.make_async_remote_copy(
            src_ref=src, dst_ref=dst, send_sem=ssem, recv_sem=rsem,
            device_id=who, device_id_type=MESH,
        )

    def send(*args):
        copy = remote(*args)
        copy.start()
        return copy

    def halo(buf, k):
        return [
            send(buf.at[pl.ds(2, 2)], buf.at[pl.ds(10, 2)], halo_s.at[k, 0], halo_r.at[k, 0], before),
            send(buf.at[pl.ds(8, 2)], buf.at[pl.ds(0, 2)], halo_s.at[k, 1], halo_r.at[k, 1], after),
        ]

    def share(buf, k):
        tile = buf.at[col]
        return [send(tile, tile, all_s.at[k, j], all_r.at[k, j], others[j]) for j in range(7)]

    def share_on(buf, k):
        tiles = buf.at[pl.ds(z_lo * 8, 8)]
        return [send(tiles, tiles, all_s.at[k, 7], all_r.at[k, 7], partner)]

    def finish(copies):
        for copy in copies:
            copy.wait()

    groups = ((red_a, g, 8, 0), (red_y, y, 4, 7), (red_z, z, 4, 10))

    def reduce_stage(rows, k, stage):
        buf, mine, size, first = groups[stage]
        buf[k, mine, pl.ds(0, 2), :] = rows
        tile = buf.at[k, mine, pl.ds(0, 2)]
        return [
            send(tile, tile, red_s.at[k, first + j], red_r.at[k, first + j], others[first + j])
            for j in range(size - 1)
        ]

    def reduce_sum(copies, k, stage):
        finish(copies)
        buf, _, size, _ = groups[stage]
        rows = buf[k, 0, pl.ds(0, 2), :]
        for i in range(1, size):
            rows = rows + buf[k, i, pl.ds(0, 2), :]
        return rows

    def reduce_begin(u, v, k):
        rows = jnp.concatenate([jnp.sum(u, axis=0, keepdims=True), jnp.sum(v, axis=0, keepdims=True)], axis=0)
        return reduce_stage(rows, k, 0)

    def reduce_on(copies, k, stage):
        return reduce_stage(reduce_sum(copies, k, stage), k, stage + 1)

    def reduce_end(copies, k):
        rows = jnp.sum(reduce_sum(copies, k, 2), axis=1, keepdims=True)
        return rows[0:1], rows[1:2]

    for s in range(8):
        for k in range(3):
            ext_c[2 + s, pl.ds(k, 1), :] = nc_ref[pl.ds(k, 1), pl.ds(s * LANES, LANES)]
        ext_c[2 + s, pl.ds(3, 5), :] = jnp.zeros((5, LANES), F32)

    slots[...] = jnp.full(slots.shape, -1, jnp.int32)
    for j in range(SLOTS // LANES):
        width = min(LANES, count - j * LANES)
        slots[pl.ds(j, 1), pl.ds(0, width)] = bnd_ref[:, pl.ds(j * LANES, width)]
    slot_ids = slots[...]
    live = jnp.where(slot_ids >= 0, 1.0, 0.0)
    tri = lax.broadcasted_iota(jnp.int32, (LANES, LANES), 0) <= lax.broadcasted_iota(jnp.int32, (LANES, LANES), 1)
    tri = jnp.where(tri, 1.0, 0.0).astype(BF16)
    rank = jnp.dot(live.astype(BF16), tri, preferred_element_type=F32) - 1.0
    totals = jnp.sum(live, axis=1, keepdims=True)
    base = jnp.zeros((1, 1), F32)
    bases = []
    for j in range(8):
        bases.append(base)
        base = base + totals[j : j + 1]
    rank = rank + jnp.concatenate(bases, axis=0)
    spot = (rank + jnp.where(rank >= MAIN, 1.0 * (WIDE - MAIN), 0.0)).astype(jnp.int32)
    spot = jnp.where(slot_ids >= 0, spot, -1)
    for j in range(SLOTS // LANES):
        line = jnp.broadcast_to(spot[j : j + 1, :], (SLOTS, LANES))
        hot = jnp.where(line == lax.broadcasted_iota(jnp.int32, (SLOTS, LANES), 0), 1.0, 0.0)
        order[:, pl.ds(j * LANES, LANES)] = hot.astype(BF16)
    tile = source.at[col]
    tile[...] = jnp.zeros((8, SLOTS), F32)
    for j in range(SLOTS // LANES):
        tile[pl.ds(0, 1), pl.ds(j * LANES, LANES)] = (slot_ids[j : j + 1, :] + 1).astype(F32)
    for k in range(3):
        tile[pl.ds(1 + k, 1), pl.ds(0, count)] = an_ref[pl.ds(k, 1), :]
    one, two, three = pieces(tile[...])
    stacked = jnp.concatenate([one, two, three, jnp.zeros((8, SLOTS), F32)], axis=0).astype(BF16)
    moved = lax.dot_general(stacked, order[...], (((1,), (1,)), ((), ())), preferred_element_type=F32)
    moved = moved[0:8] + moved[8:16] + moved[16:24]
    chosen[...] = jnp.full(chosen.shape, -1, jnp.int32)
    for j in range(SLOTS // LANES):
        chosen[pl.ds(j, 1), :] = moved[0:1, j * LANES : (j + 1) * LANES].astype(jnp.int32) - 1
    nodes = chosen[...]
    tile[pl.ds(3, 3), :] = moved[1:4]
    for k in range(3):
        tables = [jnp.broadcast_to(ext_c[2 + s, pl.ds(k, 1), :], (8, LANES)) for s in range(8)]
        where = pick(tables, nodes)
        for j in range(SLOTS // LANES):
            tile[pl.ds(k, 1), pl.ds(j * LANES, LANES)] = where[j : j + 1, :]
    near[row] = tile[:, 0:WIDE]

    pl.semaphore_wait(barrier, len(greeted))
    coords_sent = halo(ext_c, 0)
    static_sent = share(source, 0)

    def send_targets():
        for j in range(7):
            send(near.at[row], near.at[row], near_s.at[j], near_r.at[j], column[j])

        @pl.when(at_end)
        def _():
            for r in range(8):
                remote(tile.at[:, pl.ds(WIDE, WIDE)], far, far_s.at[r], far_r, helpers[r]).start()

    full = elems // LANES
    for a in range(4):
        ids[a, pl.ds(full // 8 * 8, tet_rows - full // 8 * 8), :] = jnp.full(
            (tet_rows - full // 8 * 8, LANES), -1, jnp.int32)
        for j in range(full):
            ids[a, pl.ds(j, 1), :] = tet_ref[pl.ds(a, 1), pl.ds(j * LANES, LANES)]
        rest = elems - full * LANES
        if rest:
            ids[a, pl.ds(full, 1), pl.ds(0, rest)] = tet_ref[pl.ds(a, 1), pl.ds(full * LANES, rest)]

    def build(q, carry):
        lane = lax.broadcasted_iota(jnp.int32, (LANES, LANES), 0)
        for a in range(4):
            low = jnp.broadcast_to(ids[a, pl.ds(q, 1), :] & (LANES - 1), (LANES, LANES))
            hot = jnp.where(low == lane, 1.0, 0.0).astype(BF16)
            onehot[:, pl.ds(pl.multiple_of((q * 4 + a) * LANES, LANES), LANES)] = hot
        return carry

    lax.fori_loop(0, tet_rows, build, 0)

    def node_sums(between=None):
        def spread_rows(q, carry):
            level = lax.broadcasted_iota(jnp.int32, (8, LANES), 0) + 2
            for a in range(4):
                high = jnp.broadcast_to(ids[a, pl.ds(q, 1), :] >> 7, (8, LANES))
                val = jnp.broadcast_to(vals[a, pl.ds(q, 1), :], (8, LANES))
                one, two, three = pieces(jnp.where(high == level, val, 0.0))
                block = jnp.concatenate([one, two, three, jnp.zeros((8, LANES), F32)], axis=0)
                spread[:, pl.ds(pl.multiple_of((q * 4 + a) * LANES, LANES), LANES)] = block.astype(BF16)
            return carry

        lax.fori_loop(0, tet_rows, spread_rows, 0)
        if between is not None:
            between()

        def accumulate(i, total):
            at = pl.ds(pl.multiple_of(i * CHUNK, CHUNK), CHUNK)
            return total + lax.dot_general(
                spread[:, at], onehot[:, at], (((1,), (1,)), ((), ())), preferred_element_type=F32)

        total = lax.fori_loop(0, onehot.shape[1] // CHUNK, accumulate, jnp.zeros((32, LANES), F32))
        return total[0:8] + total[8:16] + total[16:24]

    finish(coords_sent)

    def shape_elements(i, carry):
        at = pl.ds(pl.multiple_of(i * 8, 8), 8)
        corner = [ids[a, at, :] for a in range(4)]
        spots = []
        for a in range(4):
            low, high = corner[a] & (LANES - 1), corner[a] >> 7
            xyz = [jnp.zeros((8, LANES), F32) for _ in range(3)]
            for r in range(12):
                hit = high == r
                for k in range(3):
                    line = jnp.broadcast_to(ext_c[r, pl.ds(k, 1), :], (8, LANES))
                    xyz[k] = jnp.where(hit, lane_pick(line, low), xyz[k])
            spots.append(xyz)
        edges = [[spots[a][k] - spots[0][k] for k in range(3)] for a in range(1, 4)]
        n1 = cross(edges[1], edges[2])
        n2 = cross(edges[2], edges[0])
        n3 = cross(edges[0], edges[1])
        n0 = tuple(-(n1[k] + n2[k] + n3[k]) for k in range(3))
        present = corner[0] >= 0
        volume = jnp.abs(jnp.where(present, dot3(edges[0], n1), 1.0))
        weight = jnp.where(present, 1.0 / (6.0 * volume), 0.0)
        normals = (n0, n1, n2, n3)
        for e, (a, b) in enumerate(PAIRS):
            value = dot3(normals[a], normals[b]) * weight
            stiff[e, at, :] = value
            if a == b:
                vals[a, at, :] = value
        return carry

    lax.fori_loop(0, tet_rows // 8, shape_elements, 0)
    finish(static_sent)
    static_sent = share_on(source, 0)
    reaction = rea_ref[...]
    diagonal = reaction + node_sums()

    def apply(field, k, running=None):
        table = ext_v.at[k]
        for s in range(8):
            table[2 + s] = jnp.broadcast_to(field[s : s + 1, :], (8, LANES))
        finish(halo(table, 1 + k))
        if running is not None:
            running.append(reduce_on(running.pop(), k - 1, 0))

        def products(i, carry):
            at = pl.ds(pl.multiple_of(i * 8, 8), 8)
            corner = []
            for a in range(4):
                corner.append(pick([table[r] for r in range(12)], ids[a, at, :]))
            sums = [None] * 4
            for e, (a, b) in enumerate(PAIRS):
                value = stiff[e, at, :]
                for m, n in {(a, b), (b, a)}:
                    term = value * corner[n]
                    sums[m] = term if sums[m] is None else sums[m] + term
            for a in range(4):
                vals[a, at, :] = sums[a]
            return carry

        lax.fori_loop(0, tet_rows // 8, products, 0)

        def between():
            if running is not None:
                running.append(reduce_on(running.pop(), k - 1, 1))

        return reaction * field + node_sums(between)

    r = load_ref[...]
    u = r / diagonal
    w = apply(u, 0)
    x = zz = q = s_ = p = gamma_old = alpha = None
    for k in range(ITERS - 1):
        running = [reduce_begin(r * u, w * u, k)]
        m = w / diagonal
        n = apply(m, k + 1, running)
        gamma, delta = reduce_end(running.pop(), k)
        if k == 0:
            alpha = gamma / delta
            zz, q, s_, p = n, m, w, u
            x = alpha * p
        else:
            beta = gamma / gamma_old
            alpha = gamma / (delta - beta * gamma / alpha)
            zz, q, s_, p = n + beta * zz, m + beta * q, w + beta * s_, u + beta * p
            x = x + alpha * p
        r, u, w = r - alpha * s_, u - alpha * q, w - alpha * zz
        gamma_old = gamma
        if k == 0:
            send_targets()
    last = ITERS - 1
    running = reduce_begin(r * u, w * u, last)

    for i, part_of in enumerate((x, u, p)):
        tables = [jnp.broadcast_to(part_of[s : s + 1, :], (8, LANES)) for s in range(8)]
        trace[col, pl.ds(4 * i, 4), :] = pick(tables, nodes)[0:4]
    trace_sent = share(trace, 1)
    running = reduce_on(running, last, 0)

    def split_target(b, tile, first):
        t = tile[0:3] - first
        t_one, t_two, t_three = pieces(t)
        q_one, q_two, q_three = pieces(dot3((t[0:1], t[1:2], t[2:3]), (t[0:1], t[1:2], t[2:3])))
        none3, none1 = jnp.zeros((3, WIDE), F32), jnp.zeros((1, WIDE), F32)
        unit = jnp.ones((1, WIDE), F32)
        blocks_d, blocks_n = [], []
        for piece, lead in ((t_one, 1), (t_two, 0), (t_three, 0), (t_one, 1), (t_two, 0), (t_one, 1)):
            flag = unit if lead else none1
            blocks_d += [-2.0 * piece, none3, flag, none1]
            blocks_n += [none3, piece, none1, -flag]
        blocks_d += [q_one, q_two, q_three] + [none1] * 13
        blocks_n += [none1] * 16
        fill = jnp.zeros((64, WIDE), F32)
        for i, blocks in enumerate((blocks_d, blocks_n)):
            lhs[b, i] = jnp.concatenate(blocks + [fill], axis=0).T[:, 0:64].astype(BF16)

    finish(static_sent)
    for j in range(7):
        remote(near.at[row], near.at[row], near_s.at[j], near_r.at[j], column[j]).wait()
    remote(far, far, far_s.at[0], far_r, keeper).wait_recv()

    @pl.when(at_end)
    def _():
        for r in range(8):
            remote(tile.at[:, pl.ds(WIDE, WIDE)], far, far_s.at[r], far_r, helpers[r]).wait_send()

    own_first = near[row][0:3, 0:1]
    far_first = far[0:3, 0:1]

    def split_near(b, carry):
        split_target(b, near[b], own_first)
        return carry

    lax.fori_loop(0, 8, split_near, 0)
    split_target(8, far[...], far_first)

    finish(trace_sent)
    trace_sent = share_on(trace, 1)
    running = reduce_on(running, last, 1)
    gamma, delta = reduce_end(running, last)
    beta = gamma / gamma_old
    alpha = gamma / (delta - beta * gamma / alpha)
    x = x + alpha * (u + beta * p)
    sol_ref[...] = x
    tables = [jnp.broadcast_to(x[s : s + 1, :], (8, LANES)) for s in range(8)]
    own_trace = pick(tables, slot_ids)
    finish(trace_sent)

    def whole_trace(c):
        return trace[c, pl.ds(0, 4), :] + alpha * (trace[c, pl.ds(4, 4), :] + beta * trace[c, pl.ds(8, 4), :])

    def split_sources(first):
        unit = jnp.where(lax.broadcasted_iota(jnp.int32, (8, WIDE), 0) < 3, 1.0, 0.0).astype(F32)

        def put(i, tile, tr):
            s = tile[0:3] - first
            w = tile[3:6] * tr
            sx, wx = [s[k : k + 1] for k in range(3)], [w[k : k + 1] for k in range(3)]
            data = jnp.concatenate([s, w, dot3(sx, sx) + 0.25, dot3(sx, wx)], axis=0)
            one, two, three = pieces(data)
            block = jnp.concatenate([one, one, one, two, two, three, unit, jnp.zeros((8, WIDE), F32)], axis=0)
            rhs[:, pl.ds(pl.multiple_of(i * WIDE, WIDE), WIDE)] = block.astype(BF16)

        def each(c, carry):
            tr = whole_trace(c)
            put(c, source[c, :, pl.ds(0, WIDE)], jnp.concatenate([tr[0:1], tr[1:2]], axis=1))
            return carry

        lax.fori_loop(0, 16, each, 0)
        for i, c in ((16, 0), (17, 15)):
            tr = whole_trace(c)
            put(i, source[c, :, pl.ds(WIDE, WIDE)], jnp.concatenate([tr[2:3], tr[3:4]], axis=1))

    def pair_sums(b):
        parts = []
        for low, high in ((0, 128), (128, BLOCK)):
            left_d, left_n = lhs[b, 0, low:high, :], lhs[b, 1, low:high, :]

            def some(i, total):
                for u in range(UNROLL):
                    right = rhs[:, pl.ds(pl.multiple_of((i * UNROLL + u) * WIDE, WIDE), WIDE)]
                    d = jnp.dot(left_d, right, preferred_element_type=F32)
                    n = jnp.dot(left_n, right, preferred_element_type=F32)
                    inv = lax.rsqrt(d)
                    c = (n * inv) * (inv * inv)
                    total = total + (c[:, 0:LANES] + c[:, LANES:WIDE])
                return total

            parts.append(lax.fori_loop(0, 18 // UNROLL, some, jnp.zeros((high - low, LANES), F32)))
        parts.append(jnp.zeros((WIDE - BLOCK, LANES), F32))
        return jnp.sum(jnp.concatenate(parts, axis=0).T, axis=0, keepdims=True)

    def keep(ref, sums):
        ref[pl.ds(0, 1), :] = sums[:, 0:LANES]
        ref[pl.ds(1, 1), :] = sums[:, LANES:WIDE]

    split_sources(far_first)
    keep(part.at[8], pair_sums(8))
    fex_sent = send(part.at[8], fex.at[row], fex_s, fex_r.at[row], keeper)
    split_sources(own_first)

    def one_row(j, carry):
        other = (row + j) % 8
        keep(part.at[other], pair_sums(other))
        remote(part.at[other], fin.at[row], fin_s.at[j - 1], fin_r.at[j - 1], (other, col)).start()
        return carry

    lax.fori_loop(1, 8, one_row, 0)
    keep(part.at[row], pair_sums(row))
    fin[row] = part[row]
    fex_sent.wait_send()
    for j in range(7):
        remote(part.at[row], fin.at[row], fin_s.at[j], fin_r.at[j], column[j]).wait()

    @pl.when(at_end)
    def _():
        for r in range(8):
            remote(part.at[8], fex.at[r], fex_s, fex_r.at[r], keeper).wait_recv()

    total, more = fin[0], fex[0]
    for r in range(1, 8):
        total, more = total + fin[r], more + fex[r]
    tables = [jnp.broadcast_to(v[j : j + 1, :], (8, LANES)) for v in (total, more) for j in range(2)]
    result = live * (-0.5 * own_trace + (0.25 / math.pi) * pick(tables, spot))
    for j in range(SLOTS // LANES):
        width = min(LANES, count - j * LANES)
        out_ref[:, pl.ds(j * LANES, width)] = result[j : j + 1, 0:width]


def local(node_coords, tet_nodes, bnd_nodes, reaction, load, area_normal):
    elems, count = tet_nodes.shape[1], bnd_nodes.shape[0]
    tet_rows = -(-elems // 1024) * 8
    length = 4 * tet_rows * LANES
    dma = pltpu.SemaphoreType.DMA
    sol, demag = pl.pallas_call(
        full_kernel,
        out_shape=(
            jax.ShapeDtypeStruct((8, LANES), F32),
            jax.ShapeDtypeStruct((1, count), F32),
        ),
        in_specs=[VMEM] * 6,
        out_specs=(VMEM,) * 2,
        scratch_shapes=[
            pltpu.VMEM((4, tet_rows, LANES), jnp.int32),
            pltpu.VMEM((12, 8, LANES), F32),
            pltpu.VMEM((ITERS, 12, 8, LANES), F32),
            pltpu.VMEM((LANES, length), BF16),
            pltpu.VMEM((32, length), BF16),
            pltpu.VMEM((10, tet_rows, LANES), F32),
            pltpu.VMEM((4, tet_rows, LANES), F32),
            pltpu.VMEM((8, LANES), jnp.int32),
            pltpu.VMEM((8, LANES), jnp.int32),
            pltpu.VMEM((SLOTS, SLOTS), BF16),
            pltpu.VMEM((16, 8, SLOTS), F32),
            pltpu.VMEM((16, 16, LANES), F32),
            pltpu.VMEM((8, 8, WIDE), F32),
            pltpu.VMEM((8, WIDE), F32),
            pltpu.VMEM((64, 18 * WIDE), BF16),
            pltpu.VMEM((9, 2, WIDE, 64), BF16),
            pltpu.VMEM((9, 8, LANES), F32),
            pltpu.VMEM((8, 8, LANES), F32),
            pltpu.VMEM((8, 8, LANES), F32),
            pltpu.VMEM((ITERS, 8, 8, LANES), F32),
            pltpu.VMEM((ITERS, 4, 8, LANES), F32),
            pltpu.VMEM((ITERS, 4, 8, LANES), F32),
            dma((1 + ITERS, 2)), dma((1 + ITERS, 2)),
            dma((ITERS, 13)), dma((ITERS, 13)),
            dma((2, 8)), dma((2, 8)),
            dma((7,)), dma((7,)),
            dma((8,)), dma(()),
            dma((7,)), dma((7,)),
            dma(()), dma((8,)),
        ],
        compiler_params=pltpu.CompilerParams(collective_id=0, has_side_effects=True, vmem_limit_bytes=60 << 20),
        name="full",
    )(tet_nodes, node_coords, bnd_nodes.reshape(1, count), area_normal,
      reaction.reshape(8, LANES), load.reshape(8, LANES))
    return sol.reshape(-1), demag.reshape(-1)


def solution(mesh):
    placed = (
        P(None, ("row", "col")),
        P(None, ("row", "col")),
        P(("row", "col")),
        P(("row", "col")),
        P(("row", "col")),
        P(None, ("row", "col")),
    )
    return jax.shard_map(
        local,
        mesh=mesh,
        in_specs=placed,
        out_specs=(P(("row", "col")), P(("row", "col"))),
        check_vma=False,
    )
```

```python
import functools
import math

import jax
import jax.numpy as jnp
from jax import lax
from jax.experimental import pallas as pl
from jax.experimental.pallas import tpu as pltpu
from jax.sharding import PartitionSpec as P

ITERS = 3
LANES = 128
SLOTS = 512
F32 = jnp.float32
BF16 = jnp.bfloat16
MESH = pl.DeviceIdType.MESH
VMEM = pl.BlockSpec(memory_space=pltpu.VMEM)
CHUNK = 7168
QS = 16
WIDE = 256
HALF = 64
MAIN = 4 * 4 * (QS - 1)
BLOCK = 240
UNROLL = 18
PAIRS = [(a, b) for a in range(4) for b in range(a, 4)]


def place():
    row, col = lax.axis_index("row"), lax.axis_index("col")
    z_hi, y = row // 4, row % 4
    z_lo, g = col // 8, col % 8
    return row, col, z_hi, y, z_lo, g


def peers():
    row, col, z_hi, y, z_lo, g = place()
    out = [(row, z_lo * 8 + (g + j) % 8) for j in range(1, 8)]
    out += [(z_hi * 4 + (y + j) % 4, col) for j in range(1, 4)]
    z = z_hi * 2 + z_lo
    for j in range(1, 4):
        other = (z + j) % 4
        out.append(((other // 2) * 4 + y, (other % 2) * 8 + g))
    return out


def lane_pick(table, low):
    return jnp.take_along_axis(table, low, axis=1, mode="promise_in_bounds")


def pick(rows, ids):
    low = ids & (LANES - 1)
    high = ids >> 7
    out = jnp.zeros(ids.shape, F32)
    for r, row in enumerate(rows):
        out = jnp.where(high == r, lane_pick(row, low), out)
    return out


def pieces(v):
    one = v.astype(BF16).astype(F32)
    rest = v - one
    two = rest.astype(BF16).astype(F32)
    return one, two, rest - two


def cross(u, v):
    return (
        u[1] * v[2] - u[2] * v[1],
        u[2] * v[0] - u[0] * v[2],
        u[0] * v[1] - u[1] * v[0],
    )


def dot3(u, v):
    return u[0] * v[0] + u[1] * v[1] + u[2] * v[2]


def full_kernel(
    tet_ref, nc_ref, bnd_ref, an_ref, rea_ref, load_ref,
    sol_ref, out_ref,
    ids, ext_c, ext_v, onehot, spread, folded, stiff, vals, slots, chosen, order,
    source, trace, near, far, rhs, lhs, part, fin, fex,
    red_a, red_y, red_z,
    halo_s, halo_r, red_s, red_r, all_s, all_r, near_s, near_r, far_s, far_r,
    fin_s, fin_r, fex_s, fex_r,
):
    row, col, z_hi, y, z_lo, g = place()
    z = z_hi * 2 + z_lo
    others = peers()
    before, after = (row, (col + 15) % 16), (row, (col + 1) % 16)
    partner = (row, (1 - z_lo) * 8 + g)
    column = [((row + j) % 8, col) for j in range(1, 8)]
    keeper = (col % 8, (1 - col // 8) * 15)
    at_end = col % 15 == 0
    helped = row + (1 - col // 15) * 8
    helpers = [(r, helped) for r in range(8)]
    elems = tet_ref.shape[1]
    count = bnd_ref.shape[1]
    tet_rows = ids.shape[1]

    fex[...] = jnp.zeros(fex.shape, F32)
    folded[...] = jnp.zeros(folded.shape, F32)
    part[...] = jnp.zeros(part.shape, F32)

    barrier = pltpu.get_barrier_semaphore()
    greeted = others + [before, after]
    for who in greeted:
        pl.semaphore_signal(barrier, inc=1, device_id=who, device_id_type=MESH)

    def remote(src, dst, ssem, rsem, who):
        return pltpu.make_async_remote_copy(
            src_ref=src, dst_ref=dst, send_sem=ssem, recv_sem=rsem,
            device_id=who, device_id_type=MESH,
        )

    def send(*args):
        copy = remote(*args)
        copy.start()
        return copy

    def halo(buf, k):
        return [
            send(buf.at[pl.ds(2, 2)], buf.at[pl.ds(10, 2)], halo_s.at[k, 0], halo_r.at[k, 0], before),
            send(buf.at[pl.ds(8, 2)], buf.at[pl.ds(0, 2)], halo_s.at[k, 1], halo_r.at[k, 1], after),
        ]

    def share(buf, k):
        tile = buf.at[col]
        return [send(tile, tile, all_s.at[k, j], all_r.at[k, j], others[j]) for j in range(7)]

    def share_on(buf, k):
        tiles = buf.at[pl.ds(z_lo * 8, 8)]
        return [send(tiles, tiles, all_s.at[k, 7], all_r.at[k, 7], partner)]

    def finish(copies):
        for copy in copies:
            copy.wait()

    groups = ((red_a, g, 8, 0), (red_y, y, 4, 7), (red_z, z, 4, 10))

    def reduce_stage(rows, k, stage):
        buf, mine, size, first = groups[stage]
        buf[k, mine, pl.ds(0, 2), :] = rows
        tile = buf.at[k, mine, pl.ds(0, 2)]
        return [
            send(tile, tile, red_s.at[k, first + j], red_r.at[k, first + j], others[first + j])
            for j in range(size - 1)
        ]

    def reduce_sum(copies, k, stage):
        finish(copies)
        buf, _, size, _ = groups[stage]
        rows = buf[k, 0, pl.ds(0, 2), :]
        for i in range(1, size):
            rows = rows + buf[k, i, pl.ds(0, 2), :]
        return rows

    def reduce_begin(u, v, k):
        rows = jnp.concatenate([jnp.sum(u, axis=0, keepdims=True), jnp.sum(v, axis=0, keepdims=True)], axis=0)
        return reduce_stage(rows, k, 0)

    def reduce_on(copies, k, stage):
        return reduce_stage(reduce_sum(copies, k, stage), k, stage + 1)

    def reduce_end(copies, k):
        rows = jnp.sum(reduce_sum(copies, k, 2), axis=1, keepdims=True)
        return rows[0:1], rows[1:2]

    for s in range(8):
        for k in range(3):
            ext_c[2 + s, pl.ds(k, 1), :] = nc_ref[pl.ds(k, 1), pl.ds(s * LANES, LANES)]
        ext_c[2 + s, pl.ds(3, 5), :] = jnp.zeros((5, LANES), F32)

    slots[...] = jnp.full(slots.shape, -1, jnp.int32)
    for j in range(SLOTS // LANES):
        width = min(LANES, count - j * LANES)
        slots[pl.ds(j, 1), pl.ds(0, width)] = bnd_ref[:, pl.ds(j * LANES, width)]
    slot_ids = slots[...]
    live = jnp.where(slot_ids >= 0, 1.0, 0.0)
    tri = lax.broadcasted_iota(jnp.int32, (LANES, LANES), 0) <= lax.broadcasted_iota(jnp.int32, (LANES, LANES), 1)
    tri = jnp.where(tri, 1.0, 0.0).astype(BF16)
    rank = jnp.dot(live.astype(BF16), tri, preferred_element_type=F32) - 1.0
    totals = jnp.sum(live, axis=1, keepdims=True)
    base = jnp.zeros((1, 1), F32)
    bases = []
    for j in range(8):
        bases.append(base)
        base = base + totals[j : j + 1]
    rank = rank + jnp.concatenate(bases, axis=0)
    spot = (rank + jnp.where(rank >= MAIN, 1.0 * (WIDE - MAIN), 0.0)).astype(jnp.int32)
    spot = jnp.where(slot_ids >= 0, spot, -1)
    for j in range(SLOTS // LANES):
        line = jnp.broadcast_to(spot[j : j + 1, :], (SLOTS, LANES))
        hot = jnp.where(line == lax.broadcasted_iota(jnp.int32, (SLOTS, LANES), 0), 1.0, 0.0)
        order[:, pl.ds(j * LANES, LANES)] = hot.astype(BF16)
    tile = source.at[col]
    tile[...] = jnp.zeros((8, SLOTS), F32)
    for j in range(SLOTS // LANES):
        tile[pl.ds(0, 1), pl.ds(j * LANES, LANES)] = (slot_ids[j : j + 1, :] + 1).astype(F32)
    for k in range(3):
        tile[pl.ds(1 + k, 1), pl.ds(0, count)] = an_ref[pl.ds(k, 1), :]
    one, two, three = pieces(tile[...])
    stacked = jnp.concatenate([one, two, three, jnp.zeros((8, SLOTS), F32)], axis=0).astype(BF16)
    moved = lax.dot_general(stacked, order[...], (((1,), (1,)), ((), ())), preferred_element_type=F32)
    moved = moved[0:8] + moved[8:16] + moved[16:24]
    chosen[...] = jnp.full(chosen.shape, -1, jnp.int32)
    for j in range(SLOTS // LANES):
        chosen[pl.ds(j, 1), :] = moved[0:1, j * LANES : (j + 1) * LANES].astype(jnp.int32) - 1
    nodes = chosen[...]
    tile[pl.ds(3, 3), :] = moved[1:4]
    for k in range(3):
        tables = [jnp.broadcast_to(ext_c[2 + s, pl.ds(k, 1), :], (8, LANES)) for s in range(8)]
        where = pick(tables, nodes)
        for j in range(SLOTS // LANES):
            tile[pl.ds(k, 1), pl.ds(j * LANES, LANES)] = where[j : j + 1, :]
    near[row] = tile[:, 0:WIDE]

    pl.semaphore_wait(barrier, len(greeted))
    coords_sent = halo(ext_c, 0)
    static_sent = share(source, 0)

    def send_targets():
        for j in range(7):
            send(near.at[row], near.at[row], near_s.at[j], near_r.at[j], column[j])

        @pl.when(at_end)
        def _():
            for r in range(8):
                remote(tile.at[:, pl.ds(WIDE, WIDE)], far, far_s.at[r], far_r, helpers[r]).start()

    full = elems // LANES
    for a in range(4):
        ids[a, pl.ds(full // 8 * 8, tet_rows - full // 8 * 8), :] = jnp.full(
            (tet_rows - full // 8 * 8, LANES), -1, jnp.int32)
        for j in range(full):
            ids[a, pl.ds(j, 1), :] = tet_ref[pl.ds(a, 1), pl.ds(j * LANES, LANES)]
        rest = elems - full * LANES
        if rest:
            ids[a, pl.ds(full, 1), pl.ds(0, rest)] = tet_ref[pl.ds(a, 1), pl.ds(full * LANES, rest)]

    def build(q, carry):
        lane = lax.broadcasted_iota(jnp.int32, (HALF, LANES), 0)
        for a in range(4):
            low = jnp.broadcast_to(ids[a, pl.ds(q, 1), :] & (HALF - 1), (HALF, LANES))
            hot = jnp.where(low == lane, 1.0, 0.0).astype(BF16)
            onehot[:, pl.ds(pl.multiple_of((q * 4 + a) * LANES, LANES), LANES)] = hot
        return carry

    lax.fori_loop(0, tet_rows, build, 0)

    def node_sums(between=None):
        def spread_rows(q, carry):
            level = lax.broadcasted_iota(jnp.int32, (16, LANES), 0) + 4
            for a in range(4):
                high = jnp.broadcast_to(ids[a, pl.ds(q, 1), :] >> 6, (16, LANES))
                val = jnp.broadcast_to(vals[a, pl.ds(q, 1), :], (8, LANES))
                one = val.astype(BF16).astype(F32)
                hit = high == level
                two = val - one
                one, two = [jnp.where(hit, jnp.concatenate([v, v], axis=0), 0.0) for v in (one, two)]
                block = jnp.concatenate([one, two], axis=0)
                spread[:, pl.ds(pl.multiple_of((q * 4 + a) * LANES, LANES), LANES)] = block.astype(BF16)
            return carry

        lax.fori_loop(0, tet_rows, spread_rows, 0, unroll=4)
        if between is not None:
            between()

        def accumulate(i, total):
            at = pl.ds(pl.multiple_of(i * CHUNK, CHUNK), CHUNK)
            return total + lax.dot_general(
                spread[:, at], onehot[:, at], (((1,), (1,)), ((), ())), preferred_element_type=F32)

        total = lax.fori_loop(0, onehot.shape[1] // CHUNK, accumulate, jnp.zeros((32, HALF), F32))
        folded[:, pl.ds(0, HALF)] = total[0:16] + total[16:32]
        even = folded[pl.ds(0, 8, stride=2), :]
        odd = pltpu.roll(folded[pl.ds(1, 8, stride=2), :], HALF, 1)
        return jnp.where(lax.broadcasted_iota(jnp.int32, (8, LANES), 1) < HALF, even, odd)

    finish(coords_sent)

    def shape_elements(i, carry):
        at = pl.ds(pl.multiple_of(i * 8, 8), 8)
        corner = [ids[a, at, :] for a in range(4)]
        spots = []
        for a in range(4):
            low, high = corner[a] & (LANES - 1), corner[a] >> 7
            xyz = [jnp.zeros((8, LANES), F32) for _ in range(3)]
            for r in range(12):
                hit = high == r
                for k in range(3):
                    line = jnp.broadcast_to(ext_c[r, pl.ds(k, 1), :], (8, LANES))
                    xyz[k] = jnp.where(hit, lane_pick(line, low), xyz[k])
            spots.append(xyz)
        edges = [[spots[a][k] - spots[0][k] for k in range(3)] for a in range(1, 4)]
        n1 = cross(edges[1], edges[2])
        n2 = cross(edges[2], edges[0])
        n3 = cross(edges[0], edges[1])
        n0 = tuple(-(n1[k] + n2[k] + n3[k]) for k in range(3))
        present = corner[0] >= 0
        volume = jnp.abs(jnp.where(present, dot3(edges[0], n1), 1.0))
        weight = jnp.where(present, 1.0 / (6.0 * volume), 0.0)
        normals = (n0, n1, n2, n3)
        for e, (a, b) in enumerate(PAIRS):
            value = dot3(normals[a], normals[b]) * weight
            stiff[e, at, :] = value
            if a == b:
                vals[a, at, :] = value
        return carry

    lax.fori_loop(0, tet_rows // 8, shape_elements, 0)
    finish(static_sent)
    static_sent = share_on(source, 0)
    reaction = rea_ref[...]
    diagonal = reaction + node_sums()

    def apply(field, k, running=None):
        table = ext_v.at[k]
        for s in range(8):
            table[2 + s] = jnp.broadcast_to(field[s : s + 1, :], (8, LANES))
        finish(halo(table, 1 + k))
        if running is not None:
            running.append(reduce_on(running.pop(), k - 1, 0))

        def products(i, carry):
            at = pl.ds(pl.multiple_of(i * 8, 8), 8)
            corner = []
            for a in range(4):
                corner.append(pick([table[r] for r in range(12)], ids[a, at, :]))
            sums = [None] * 4
            for e, (a, b) in enumerate(PAIRS):
                value = stiff[e, at, :]
                for m, n in {(a, b), (b, a)}:
                    term = value * corner[n]
                    sums[m] = term if sums[m] is None else sums[m] + term
            for a in range(4):
                vals[a, at, :] = sums[a]
            return carry

        lax.fori_loop(0, tet_rows // 8, products, 0, unroll=True)

        def between():
            if running is not None:
                running.append(reduce_on(running.pop(), k - 1, 1))

        return reaction * field + node_sums(between)

    r = load_ref[...]
    u = r / diagonal
    w = apply(u, 0)
    x = zz = q = s_ = p = gamma_old = alpha = None
    for k in range(ITERS - 1):
        running = [reduce_begin(r * u, w * u, k)]
        m = w / diagonal
        n = apply(m, k + 1, running)
        gamma, delta = reduce_end(running.pop(), k)
        if k == 0:
            alpha = gamma / delta
            zz, q, s_, p = n, m, w, u
            x = alpha * p
        else:
            beta = gamma / gamma_old
            alpha = gamma / (delta - beta * gamma / alpha)
            zz, q, s_, p = n + beta * zz, m + beta * q, w + beta * s_, u + beta * p
            x = x + alpha * p
        r, u, w = r - alpha * s_, u - alpha * q, w - alpha * zz
        gamma_old = gamma
        if k == 0:
            send_targets()
    last = ITERS - 1
    running = reduce_begin(r * u, w * u, last)

    for i, part_of in enumerate((x, u, p)):
        tables = [jnp.broadcast_to(part_of[s : s + 1, :], (8, LANES)) for s in range(8)]
        trace[col, pl.ds(4 * i, 4), :] = pick(tables, nodes)[0:4]
    trace_sent = share(trace, 1)
    running = reduce_on(running, last, 0)

    def split_target(b, tile, first):
        t = tile[0:3] - first
        t_one, t_two, t_three = pieces(t)
        q_one, q_two, q_three = pieces(dot3((t[0:1], t[1:2], t[2:3]), (t[0:1], t[1:2], t[2:3])))
        none3, none1 = jnp.zeros((3, WIDE), F32), jnp.zeros((1, WIDE), F32)
        unit = jnp.ones((1, WIDE), F32)
        blocks_d, blocks_n = [], []
        for piece, lead in ((t_one, 1), (t_two, 0), (t_three, 0), (t_one, 1), (t_two, 0), (t_one, 1)):
            flag = unit if lead else none1
            blocks_d += [-2.0 * piece, none3, flag, none1]
            blocks_n += [none3, piece, none1, -flag]
        blocks_d += [q_one, q_two, q_three] + [none1] * 13
        blocks_n += [none1] * 16
        fill = jnp.zeros((64, WIDE), F32)
        for i, blocks in enumerate((blocks_d, blocks_n)):
            lhs[b, i] = jnp.concatenate(blocks + [fill], axis=0).T[:, 0:64].astype(BF16)

    finish(static_sent)
    for j in range(7):
        remote(near.at[row], near.at[row], near_s.at[j], near_r.at[j], column[j]).wait()
    remote(far, far, far_s.at[0], far_r, keeper).wait_recv()

    @pl.when(at_end)
    def _():
        for r in range(8):
            remote(tile.at[:, pl.ds(WIDE, WIDE)], far, far_s.at[r], far_r, helpers[r]).wait_send()

    own_first = near[row][0:3, 0:1]
    far_first = far[0:3, 0:1]

    def split_near(b, carry):
        split_target(b, near[b], own_first)
        return carry

    lax.fori_loop(0, 8, split_near, 0)
    split_target(8, far[...], far_first)

    finish(trace_sent)
    trace_sent = share_on(trace, 1)
    running = reduce_on(running, last, 1)
    gamma, delta = reduce_end(running, last)
    beta = gamma / gamma_old
    alpha = gamma / (delta - beta * gamma / alpha)
    x = x + alpha * (u + beta * p)
    sol_ref[...] = x
    tables = [jnp.broadcast_to(x[s : s + 1, :], (8, LANES)) for s in range(8)]
    own_trace = pick(tables, slot_ids)
    finish(trace_sent)

    def whole_trace(c):
        return trace[c, pl.ds(0, 4), :] + alpha * (trace[c, pl.ds(4, 4), :] + beta * trace[c, pl.ds(8, 4), :])

    def split_sources(kind, first):
        unit = jnp.where(lax.broadcasted_iota(jnp.int32, (8, WIDE), 0) < 3, 1.0, 0.0).astype(F32)

        def put(i, tile, tr):
            s = tile[0:3] - first
            w = tile[3:6] * tr
            sx, wx = [s[k : k + 1] for k in range(3)], [w[k : k + 1] for k in range(3)]
            data = jnp.concatenate([s, w, dot3(sx, sx) + 0.25, dot3(sx, wx)], axis=0)
            one, two, three = pieces(data)
            block = jnp.concatenate([one, one, one, two, two, three, unit, jnp.zeros((8, WIDE), F32)], axis=0)
            rhs[kind, :, pl.ds(pl.multiple_of(i * WIDE, WIDE), WIDE)] = block.astype(BF16)

        def each(c, carry):
            tr = whole_trace(c)
            put(c, source[c, :, pl.ds(0, WIDE)], jnp.concatenate([tr[0:1], tr[1:2]], axis=1))
            return carry

        lax.fori_loop(0, 16, each, 0)
        for i, c in ((16, 0), (17, 15)):
            tr = whole_trace(c)
            put(i, source[c, :, pl.ds(WIDE, WIDE)], jnp.concatenate([tr[2:3], tr[3:4]], axis=1))

    def pair_sums(b, kind):
        parts = []
        for low, high in ((0, 128), (128, BLOCK)):
            left_d, left_n = lhs[b, 0, low:high, :], lhs[b, 1, low:high, :]

            def some(i, total):
                for u in range(UNROLL):
                    right = rhs[kind, :, pl.ds(pl.multiple_of((i * UNROLL + u) * WIDE, WIDE), WIDE)]
                    d = jnp.dot(left_d, right, preferred_element_type=F32)
                    n = jnp.dot(left_n, right, preferred_element_type=F32)
                    inv = lax.rsqrt(d)
                    c = (n * inv) * (inv * inv)
                    total = total + (c[:, 0:LANES] + c[:, LANES:WIDE])
                return total

            parts.append(lax.fori_loop(0, 18 // UNROLL, some, jnp.zeros((high - low, LANES), F32)))
        parts.append(jnp.zeros((WIDE - BLOCK, LANES), F32))
        return jnp.sum(jnp.concatenate(parts, axis=0).T, axis=0, keepdims=True)

    def keep(ref, sums):
        ref[pl.ds(0, 1), :] = sums[:, 0:LANES]
        ref[pl.ds(1, 1), :] = sums[:, LANES:WIDE]

    split_sources(0, far_first)
    split_sources(1, own_first)

    def one_block(j, carry):
        other = (row + j) % 8
        b = jnp.where(j == 0, 8, other)
        keep(part.at[b], pair_sums(b, jnp.minimum(j, 1)))

        @pl.when(j == 0)
        def _():
            remote(part.at[8], fex.at[row], fex_s, fex_r.at[row], keeper).start()

        @pl.when(jnp.logical_and(j > 0, j < 8))
        def _():
            remote(part.at[other], fin.at[row], fin_s.at[j - 1], fin_r.at[j - 1], (other, col)).start()

        return carry

    lax.fori_loop(0, 9, one_block, 0)
    fin[row] = part[row]
    remote(part.at[8], fex.at[row], fex_s, fex_r.at[row], keeper).wait_send()
    for j in range(7):
        remote(part.at[row], fin.at[row], fin_s.at[j], fin_r.at[j], column[j]).wait()

    @pl.when(at_end)
    def _():
        for r in range(8):
            remote(part.at[8], fex.at[r], fex_s, fex_r.at[r], keeper).wait_recv()

    total, more = fin[0], fex[0]
    for r in range(1, 8):
        total, more = total + fin[r], more + fex[r]
    tables = [jnp.broadcast_to(v[j : j + 1, :], (8, LANES)) for v in (total, more) for j in range(2)]
    result = live * (-0.5 * own_trace + (0.25 / math.pi) * pick(tables, spot))
    for j in range(SLOTS // LANES):
        width = min(LANES, count - j * LANES)
        out_ref[:, pl.ds(j * LANES, width)] = result[j : j + 1, 0:width]


def local(node_coords, tet_nodes, bnd_nodes, reaction, load, area_normal):
    elems, count = tet_nodes.shape[1], bnd_nodes.shape[0]
    tet_rows = -(-elems // 1024) * 8
    length = 4 * tet_rows * LANES
    dma = pltpu.SemaphoreType.DMA
    sol, demag = pl.pallas_call(
        full_kernel,
        out_shape=(
            jax.ShapeDtypeStruct((8, LANES), F32),
            jax.ShapeDtypeStruct((1, count), F32),
        ),
        in_specs=[VMEM] * 6,
        out_specs=(VMEM,) * 2,
        scratch_shapes=[
            pltpu.VMEM((4, tet_rows, LANES), jnp.int32),
            pltpu.VMEM((12, 8, LANES), F32),
            pltpu.VMEM((ITERS, 12, 8, LANES), F32),
            pltpu.VMEM((HALF, length), BF16),
            pltpu.VMEM((32, length), BF16),
            pltpu.VMEM((16, LANES), F32),
            pltpu.VMEM((10, tet_rows, LANES), F32),
            pltpu.VMEM((4, tet_rows, LANES), F32),
            pltpu.VMEM((8, LANES), jnp.int32),
            pltpu.VMEM((8, LANES), jnp.int32),
            pltpu.VMEM((SLOTS, SLOTS), BF16),
            pltpu.VMEM((16, 8, SLOTS), F32),
            pltpu.VMEM((16, 16, LANES), F32),
            pltpu.VMEM((8, 8, WIDE), F32),
            pltpu.VMEM((8, WIDE), F32),
            pltpu.VMEM((2, 64, 18 * WIDE), BF16),
            pltpu.VMEM((9, 2, WIDE, 64), BF16),
            pltpu.VMEM((9, 8, LANES), F32),
            pltpu.VMEM((8, 8, LANES), F32),
            pltpu.VMEM((8, 8, LANES), F32),
            pltpu.VMEM((ITERS, 8, 8, LANES), F32),
            pltpu.VMEM((ITERS, 4, 8, LANES), F32),
            pltpu.VMEM((ITERS, 4, 8, LANES), F32),
            dma((1 + ITERS, 2)), dma((1 + ITERS, 2)),
            dma((ITERS, 13)), dma((ITERS, 13)),
            dma((2, 8)), dma((2, 8)),
            dma((7,)), dma((7,)),
            dma((8,)), dma(()),
            dma((7,)), dma((7,)),
            dma(()), dma((8,)),
        ],
        compiler_params=pltpu.CompilerParams(collective_id=0, has_side_effects=True, vmem_limit_bytes=60 << 20),
        name="full",
    )(tet_nodes, node_coords, bnd_nodes.reshape(1, count), area_normal,
      reaction.reshape(8, LANES), load.reshape(8, LANES))
    return sol.reshape(-1), demag.reshape(-1)


def solution(mesh):
    placed = (
        P(None, ("row", "col")),
        P(None, ("row", "col")),
        P(("row", "col")),
        P(("row", "col")),
        P(("row", "col")),
        P(None, ("row", "col")),
    )
    return jax.shard_map(
        local,
        mesh=mesh,
        in_specs=placed,
        out_specs=(P(("row", "col")), P(("row", "col"))),
        check_vma=False,
    )
```

```python
import functools
import math

import jax
import jax.numpy as jnp
from jax import lax
from jax.experimental import pallas as pl
from jax.experimental.pallas import tpu as pltpu
from jax.sharding import PartitionSpec as P

ITERS = 3
LANES = 128
SLOTS = 512
F32 = jnp.float32
BF16 = jnp.bfloat16
MESH = pl.DeviceIdType.MESH
VMEM = pl.BlockSpec(memory_space=pltpu.VMEM)
CHUNK = 7168
QS = 16
WIDE = 256
HALF = 64
MAIN = 4 * 4 * (QS - 1)
BLOCK = 240
UNROLL = 18
PAIRS = [(a, b) for a in range(4) for b in range(a, 4)]


def place():
    row, col = lax.axis_index("row"), lax.axis_index("col")
    z_hi, y = row // 4, row % 4
    z_lo, g = col // 8, col % 8
    return row, col, z_hi, y, z_lo, g


def peers():
    row, col, z_hi, y, z_lo, g = place()
    out = [(row, z_lo * 8 + (g + j) % 8) for j in range(1, 8)]
    plane = (z_hi * 2 + z_lo) * 4 + y
    for j in range(1, 16):
        other = (plane + j) % 16
        z = other // 4
        out.append(((z // 2) * 4 + other % 4, (z % 2) * 8 + g))
    return out


def lane_pick(table, low):
    return jnp.take_along_axis(table, low, axis=1, mode="promise_in_bounds")


def pick(rows, ids):
    low = ids & (LANES - 1)
    high = ids >> 7
    out = jnp.zeros(ids.shape, F32)
    for r, row in enumerate(rows):
        out = jnp.where(high == r, lane_pick(row, low), out)
    return out


def pieces(v):
    one = v.astype(BF16).astype(F32)
    rest = v - one
    two = rest.astype(BF16).astype(F32)
    return one, two, rest - two


def cross(u, v):
    return (
        u[1] * v[2] - u[2] * v[1],
        u[2] * v[0] - u[0] * v[2],
        u[0] * v[1] - u[1] * v[0],
    )


def dot3(u, v):
    return u[0] * v[0] + u[1] * v[1] + u[2] * v[2]


def full_kernel(
    tet_ref, nc_ref, bnd_ref, an_ref, rea_ref, load_ref,
    sol_ref, out_ref,
    ids, ext_c, ext_v, onehot, spread, folded, stiff, vals, slots, chosen, order,
    source, trace, near, far, rhs, lhs, part, fin, fex,
    red_a, red_b,
    halo_s, halo_r, red_s, red_r, all_s, all_r, near_s, near_r, far_s, far_r,
    fin_s, fin_r, fex_s, fex_r,
):
    row, col, z_hi, y, z_lo, g = place()
    z = z_hi * 2 + z_lo
    others = peers()
    before, after = (row, (col + 15) % 16), (row, (col + 1) % 16)
    partner = (row, (1 - z_lo) * 8 + g)
    column = [((row + j) % 8, col) for j in range(1, 8)]
    keeper = (col % 8, (1 - col // 8) * 15)
    at_end = col % 15 == 0
    helped = row + (1 - col // 15) * 8
    helpers = [(r, helped) for r in range(8)]
    elems = tet_ref.shape[1]
    count = bnd_ref.shape[1]
    tet_rows = ids.shape[1]

    fex[...] = jnp.zeros(fex.shape, F32)
    folded[...] = jnp.zeros(folded.shape, F32)
    part[...] = jnp.zeros(part.shape, F32)

    barrier = pltpu.get_barrier_semaphore()
    greeted = others + [before, after]
    for who in greeted:
        pl.semaphore_signal(barrier, inc=1, device_id=who, device_id_type=MESH)

    def remote(src, dst, ssem, rsem, who):
        return pltpu.make_async_remote_copy(
            src_ref=src, dst_ref=dst, send_sem=ssem, recv_sem=rsem,
            device_id=who, device_id_type=MESH,
        )

    def send(*args):
        copy = remote(*args)
        copy.start()
        return copy

    def halo(buf, k):
        return [
            send(buf.at[pl.ds(2, 2)], buf.at[pl.ds(10, 2)], halo_s.at[k, 0], halo_r.at[k, 0], before),
            send(buf.at[pl.ds(8, 2)], buf.at[pl.ds(0, 2)], halo_s.at[k, 1], halo_r.at[k, 1], after),
        ]

    shared = (8, 12)

    def share(buf, k):
        tile = buf.at[col, pl.ds(0, shared[k])]
        return [send(tile, tile, all_s.at[k, j], all_r.at[k, j], others[j]) for j in range(7)]

    def share_on(buf, k):
        tiles = buf.at[pl.ds(z_lo * 8, 8), pl.ds(0, shared[k])]
        return [send(tiles, tiles, all_s.at[k, 7], all_r.at[k, 7], partner)]

    def finish(copies):
        for copy in copies:
            copy.wait()

    groups = ((red_a, g, 8, 0), (red_b, z * 4 + y, 16, 7))

    def reduce_stage(rows, k, stage):
        buf, mine, size, first = groups[stage]
        buf[k, mine, pl.ds(0, 2), :] = rows
        tile = buf.at[k, mine, pl.ds(0, 2)]
        return [
            send(tile, tile, red_s.at[k, first + j], red_r.at[k, first + j], others[first + j])
            for j in range(size - 1)
        ]

    def reduce_sum(copies, k, stage):
        finish(copies)
        buf, _, size, _ = groups[stage]
        rows = buf[k, 0, pl.ds(0, 2), :]
        for i in range(1, size):
            rows = rows + buf[k, i, pl.ds(0, 2), :]
        return rows

    def reduce_begin(u, v, k):
        rows = jnp.concatenate([jnp.sum(u, axis=0, keepdims=True), jnp.sum(v, axis=0, keepdims=True)], axis=0)
        return reduce_stage(rows, k, 0)

    def reduce_on(copies, k, stage):
        return reduce_stage(reduce_sum(copies, k, stage), k, stage + 1)

    def reduce_end(copies, k):
        rows = jnp.sum(reduce_sum(copies, k, 1), axis=1, keepdims=True)
        return rows[0:1], rows[1:2]

    for s in range(8):
        for k in range(3):
            ext_c[2 + s, pl.ds(k, 1), :] = nc_ref[pl.ds(k, 1), pl.ds(s * LANES, LANES)]
        ext_c[2 + s, pl.ds(3, 5), :] = jnp.zeros((5, LANES), F32)

    slots[...] = jnp.full(slots.shape, -1, jnp.int32)
    for j in range(SLOTS // LANES):
        width = min(LANES, count - j * LANES)
        slots[pl.ds(j, 1), pl.ds(0, width)] = bnd_ref[:, pl.ds(j * LANES, width)]
    slot_ids = slots[...]
    live = jnp.where(slot_ids >= 0, 1.0, 0.0)
    tri = lax.broadcasted_iota(jnp.int32, (LANES, LANES), 0) <= lax.broadcasted_iota(jnp.int32, (LANES, LANES), 1)
    tri = jnp.where(tri, 1.0, 0.0).astype(BF16)
    rank = jnp.dot(live.astype(BF16), tri, preferred_element_type=F32) - 1.0
    totals = jnp.sum(live, axis=1, keepdims=True)
    base = jnp.zeros((1, 1), F32)
    bases = []
    for j in range(8):
        bases.append(base)
        base = base + totals[j : j + 1]
    rank = rank + jnp.concatenate(bases, axis=0)
    spot = (rank + jnp.where(rank >= MAIN, 1.0 * (WIDE - MAIN), 0.0)).astype(jnp.int32)
    spot = jnp.where(slot_ids >= 0, spot, -1)
    for j in range(SLOTS // LANES):
        line = jnp.broadcast_to(spot[j : j + 1, :], (SLOTS, LANES))
        hot = jnp.where(line == lax.broadcasted_iota(jnp.int32, (SLOTS, LANES), 0), 1.0, 0.0)
        order[:, pl.ds(j * LANES, LANES)] = hot.astype(BF16)
    tile = source.at[col]
    tile[...] = jnp.zeros((8, SLOTS), F32)
    for j in range(SLOTS // LANES):
        tile[pl.ds(0, 1), pl.ds(j * LANES, LANES)] = (slot_ids[j : j + 1, :] + 1).astype(F32)
    for k in range(3):
        tile[pl.ds(1 + k, 1), pl.ds(0, count)] = an_ref[pl.ds(k, 1), :]
    one, two, three = pieces(tile[...])
    stacked = jnp.concatenate([one, two, three, jnp.zeros((8, SLOTS), F32)], axis=0).astype(BF16)
    moved = lax.dot_general(stacked, order[...], (((1,), (1,)), ((), ())), preferred_element_type=F32)
    moved = moved[0:8] + moved[8:16] + moved[16:24]
    chosen[...] = jnp.full(chosen.shape, -1, jnp.int32)
    for j in range(SLOTS // LANES):
        chosen[pl.ds(j, 1), :] = moved[0:1, j * LANES : (j + 1) * LANES].astype(jnp.int32) - 1
    nodes = chosen[...]
    tile[pl.ds(3, 3), :] = moved[1:4]
    for k in range(3):
        tables = [jnp.broadcast_to(ext_c[2 + s, pl.ds(k, 1), :], (8, LANES)) for s in range(8)]
        where = pick(tables, nodes)
        for j in range(SLOTS // LANES):
            tile[pl.ds(k, 1), pl.ds(j * LANES, LANES)] = where[j : j + 1, :]
    near[row] = tile[:, 0:WIDE]

    pl.semaphore_wait(barrier, len(greeted))
    coords_sent = halo(ext_c, 0)
    static_sent = share(source, 0)

    def send_targets():
        for j in range(7):
            send(near.at[row], near.at[row], near_s.at[j], near_r.at[j], column[j])

        @pl.when(at_end)
        def _():
            for r in range(8):
                remote(tile.at[:, pl.ds(WIDE, WIDE)], far, far_s.at[r], far_r, helpers[r]).start()

    full = elems // LANES
    for a in range(4):
        ids[a, pl.ds(full // 8 * 8, tet_rows - full // 8 * 8), :] = jnp.full(
            (tet_rows - full // 8 * 8, LANES), -1, jnp.int32)
        for j in range(full):
            ids[a, pl.ds(j, 1), :] = tet_ref[pl.ds(a, 1), pl.ds(j * LANES, LANES)]
        rest = elems - full * LANES
        if rest:
            ids[a, pl.ds(full, 1), pl.ds(0, rest)] = tet_ref[pl.ds(a, 1), pl.ds(full * LANES, rest)]

    def build(q, carry):
        lane = lax.broadcasted_iota(jnp.int32, (HALF, LANES), 0)
        for a in range(4):
            low = jnp.broadcast_to(ids[a, pl.ds(q, 1), :] & (HALF - 1), (HALF, LANES))
            hot = jnp.where(low == lane, 1.0, 0.0).astype(BF16)
            onehot[:, pl.ds(pl.multiple_of((q * 4 + a) * LANES, LANES), LANES)] = hot
        return carry

    lax.fori_loop(0, tet_rows, build, 0)

    def node_sums():
        def spread_rows(q, carry):
            level = lax.broadcasted_iota(jnp.int32, (16, LANES), 0) + 4
            for a in range(4):
                high = jnp.broadcast_to(ids[a, pl.ds(q, 1), :] >> 6, (16, LANES))
                val = jnp.broadcast_to(vals[a, pl.ds(q, 1), :], (8, LANES))
                one = val.astype(BF16).astype(F32)
                hit = high == level
                two = val - one
                one, two = [jnp.where(hit, jnp.concatenate([v, v], axis=0), 0.0) for v in (one, two)]
                block = jnp.concatenate([one, two], axis=0)
                spread[:, pl.ds(pl.multiple_of((q * 4 + a) * LANES, LANES), LANES)] = block.astype(BF16)
            return carry

        lax.fori_loop(0, tet_rows, spread_rows, 0, unroll=4)

        def accumulate(i, total):
            at = pl.ds(pl.multiple_of(i * CHUNK, CHUNK), CHUNK)
            return total + lax.dot_general(
                spread[:, at], onehot[:, at], (((1,), (1,)), ((), ())), preferred_element_type=F32)

        total = lax.fori_loop(0, onehot.shape[1] // CHUNK, accumulate, jnp.zeros((32, HALF), F32))
        folded[:, pl.ds(0, HALF)] = total[0:16] + total[16:32]
        even = folded[pl.ds(0, 8, stride=2), :]
        odd = pltpu.roll(folded[pl.ds(1, 8, stride=2), :], HALF, 1)
        return jnp.where(lax.broadcasted_iota(jnp.int32, (8, LANES), 1) < HALF, even, odd)

    finish(coords_sent)

    def shape_elements(i, carry):
        at = pl.ds(pl.multiple_of(i * 8, 8), 8)
        corner = [ids[a, at, :] for a in range(4)]
        spots = []
        for a in range(4):
            low, high = corner[a] & (LANES - 1), corner[a] >> 7
            xyz = [jnp.zeros((8, LANES), F32) for _ in range(3)]
            for r in range(12):
                hit = high == r
                for k in range(3):
                    line = jnp.broadcast_to(ext_c[r, pl.ds(k, 1), :], (8, LANES))
                    xyz[k] = jnp.where(hit, lane_pick(line, low), xyz[k])
            spots.append(xyz)
        edges = [[spots[a][k] - spots[0][k] for k in range(3)] for a in range(1, 4)]
        n1 = cross(edges[1], edges[2])
        n2 = cross(edges[2], edges[0])
        n3 = cross(edges[0], edges[1])
        n0 = tuple(-(n1[k] + n2[k] + n3[k]) for k in range(3))
        present = corner[0] >= 0
        volume = jnp.abs(jnp.where(present, dot3(edges[0], n1), 1.0))
        weight = jnp.where(present, 1.0 / (6.0 * volume), 0.0)
        normals = (n0, n1, n2, n3)
        for e, (a, b) in enumerate(PAIRS):
            value = dot3(normals[a], normals[b]) * weight
            stiff[e, at, :] = value
            if a == b:
                vals[a, at, :] = value
        return carry

    lax.fori_loop(0, tet_rows // 8, shape_elements, 0)
    reaction = rea_ref[...]
    diagonal = reaction + node_sums()

    def apply(field, k, running=None):
        table = ext_v.at[k]
        for s in range(8):
            table[2 + s] = jnp.broadcast_to(field[s : s + 1, :], (8, LANES))
        finish(halo(table, 1 + k))
        if running is not None:
            running.append(reduce_on(running.pop(), k - 1, 0))

        def products(i, carry):
            at = pl.ds(pl.multiple_of(i * 8, 8), 8)
            corner = []
            for a in range(4):
                corner.append(pick([table[r] for r in range(12)], ids[a, at, :]))
            sums = [None] * 4
            for e, (a, b) in enumerate(PAIRS):
                value = stiff[e, at, :]
                for m, n in {(a, b), (b, a)}:
                    term = value * corner[n]
                    sums[m] = term if sums[m] is None else sums[m] + term
            for a in range(4):
                vals[a, at, :] = sums[a]
            return carry

        lax.fori_loop(0, tet_rows // 8, products, 0, unroll=True)

        return reaction * field + node_sums()

    r = load_ref[...]
    u = r / diagonal
    w = apply(u, 0)
    x = zz = q = s_ = p = gamma_old = alpha = None
    for k in range(ITERS - 1):
        running = [reduce_begin(r * u, w * u, k)]
        m = w / diagonal
        n = apply(m, k + 1, running)
        gamma, delta = reduce_end(running.pop(), k)
        if k == 0:
            alpha = gamma / delta
            zz, q, s_, p = n, m, w, u
            x = alpha * p
        else:
            beta = gamma / gamma_old
            alpha = gamma / (delta - beta * gamma / alpha)
            zz, q, s_, p = n + beta * zz, m + beta * q, w + beta * s_, u + beta * p
            x = x + alpha * p
        r, u, w = r - alpha * s_, u - alpha * q, w - alpha * zz
        gamma_old = gamma
        if k == 0:
            send_targets()
            finish(static_sent)
            static_sent = share_on(source, 0)
    last = ITERS - 1
    running = reduce_begin(r * u, w * u, last)

    for i, part_of in enumerate((x, u, p)):
        tables = [jnp.broadcast_to(part_of[s : s + 1, :], (8, LANES)) for s in range(8)]
        trace[col, pl.ds(4 * i, 4), :] = pick(tables, nodes)[0:4]
    trace_sent = share(trace, 1)
    running = reduce_on(running, last, 0)

    def split_target(b, tile, first):
        t = tile[0:3] - first
        t_one, t_two, t_three = pieces(t)
        q_one, q_two, q_three = pieces(dot3((t[0:1], t[1:2], t[2:3]), (t[0:1], t[1:2], t[2:3])))
        none3, none1 = jnp.zeros((3, WIDE), F32), jnp.zeros((1, WIDE), F32)
        unit = jnp.ones((1, WIDE), F32)
        blocks_d, blocks_n = [], []
        for piece, lead in ((t_one, 1), (t_two, 0), (t_three, 0), (t_one, 1), (t_two, 0), (t_one, 1)):
            flag = unit if lead else none1
            blocks_d += [-2.0 * piece, none3, flag, none1]
            blocks_n += [none3, piece, none1, -flag]
        blocks_d += [q_one, q_two, q_three] + [none1] * 13
        blocks_n += [none1] * 16
        fill = jnp.zeros((64, WIDE), F32)
        for i, blocks in enumerate((blocks_d, blocks_n)):
            lhs[b, i] = jnp.concatenate(blocks + [fill], axis=0).T[:, 0:64].astype(BF16)

    finish(static_sent)
    for j in range(7):
        remote(near.at[row], near.at[row], near_s.at[j], near_r.at[j], column[j]).wait()
    remote(far, far, far_s.at[0], far_r, keeper).wait_recv()

    @pl.when(at_end)
    def _():
        for r in range(8):
            remote(tile.at[:, pl.ds(WIDE, WIDE)], far, far_s.at[r], far_r, helpers[r]).wait_send()

    own_first = near[row][0:3, 0:1]
    far_first = far[0:3, 0:1]

    def split_near(b, carry):
        split_target(b, near[b], own_first)
        return carry

    lax.fori_loop(0, 8, split_near, 0)
    split_target(8, far[...], far_first)

    finish(trace_sent)
    trace_sent = share_on(trace, 1)
    gamma, delta = reduce_end(running, last)
    beta = gamma / gamma_old
    alpha = gamma / (delta - beta * gamma / alpha)
    x = x + alpha * (u + beta * p)
    sol_ref[...] = x
    tables = [jnp.broadcast_to(x[s : s + 1, :], (8, LANES)) for s in range(8)]
    own_trace = pick(tables, slot_ids)
    finish(trace_sent)

    def whole_trace(c):
        return trace[c, pl.ds(0, 4), :] + alpha * (trace[c, pl.ds(4, 4), :] + beta * trace[c, pl.ds(8, 4), :])

    def split_sources(kind, first):
        unit = jnp.where(lax.broadcasted_iota(jnp.int32, (8, WIDE), 0) < 3, 1.0, 0.0).astype(F32)

        def put(i, tile, tr):
            s = tile[0:3] - first
            w = tile[3:6] * tr
            sx, wx = [s[k : k + 1] for k in range(3)], [w[k : k + 1] for k in range(3)]
            data = jnp.concatenate([s, w, dot3(sx, sx) + 0.25, dot3(sx, wx)], axis=0)
            one, two, three = pieces(data)
            block = jnp.concatenate([one, one, one, two, two, three, unit, jnp.zeros((8, WIDE), F32)], axis=0)
            rhs[kind, :, pl.ds(pl.multiple_of(i * WIDE, WIDE), WIDE)] = block.astype(BF16)

        def each(c, carry):
            tr = whole_trace(c)
            put(c, source[c, :, pl.ds(0, WIDE)], jnp.concatenate([tr[0:1], tr[1:2]], axis=1))
            return carry

        lax.fori_loop(0, 16, each, 0)
        for i, c in ((16, 0), (17, 15)):
            tr = whole_trace(c)
            put(i, source[c, :, pl.ds(WIDE, WIDE)], jnp.concatenate([tr[2:3], tr[3:4]], axis=1))

    def pair_sums(b, kind):
        parts = []
        for low, high in ((0, BLOCK),):
            left_d, left_n = lhs[b, 0, low:high, :], lhs[b, 1, low:high, :]

            def some(i, total):
                for u in range(UNROLL):
                    right = rhs[kind, :, pl.ds(pl.multiple_of((i * UNROLL + u) * WIDE, WIDE), WIDE)]
                    d = jnp.dot(left_d, right, preferred_element_type=F32)
                    n = jnp.dot(left_n, right, preferred_element_type=F32)
                    inv = lax.rsqrt(d)
                    c = (n * inv) * (inv * inv)
                    total = total + (c[:, 0:LANES] + c[:, LANES:WIDE])
                return total

            parts.append(lax.fori_loop(0, 18 // UNROLL, some, jnp.zeros((high - low, LANES), F32)))
        parts.append(jnp.zeros((WIDE - BLOCK, LANES), F32))
        return jnp.sum(jnp.concatenate(parts, axis=0).T, axis=0, keepdims=True)

    def keep(ref, sums):
        ref[pl.ds(0, 1), :] = sums[:, 0:LANES]
        ref[pl.ds(1, 1), :] = sums[:, LANES:WIDE]

    split_sources(0, far_first)
    split_sources(1, own_first)

    def one_block(j, carry):
        other = (row + j) % 8
        b = jnp.where(j == 0, 8, other)
        keep(part.at[b], pair_sums(b, jnp.minimum(j, 1)))

        @pl.when(j == 0)
        def _():
            remote(part.at[8], fex.at[row], fex_s, fex_r.at[row], keeper).start()

        @pl.when(jnp.logical_and(j > 0, j < 8))
        def _():
            remote(part.at[other], fin.at[row], fin_s.at[j - 1], fin_r.at[j - 1], (other, col)).start()

        return carry

    lax.fori_loop(0, 9, one_block, 0)
    fin[row] = part[row]
    remote(part.at[8], fex.at[row], fex_s, fex_r.at[row], keeper).wait_send()
    for j in range(7):
        remote(part.at[row], fin.at[row], fin_s.at[j], fin_r.at[j], column[j]).wait()

    @pl.when(at_end)
    def _():
        for r in range(8):
            remote(part.at[8], fex.at[r], fex_s, fex_r.at[r], keeper).wait_recv()

    total, more = fin[0], fex[0]
    for r in range(1, 8):
        total, more = total + fin[r], more + fex[r]
    tables = [jnp.broadcast_to(v[j : j + 1, :], (8, LANES)) for v in (total, more) for j in range(2)]
    result = live * (-0.5 * own_trace + (0.25 / math.pi) * pick(tables, spot))
    for j in range(SLOTS // LANES):
        width = min(LANES, count - j * LANES)
        out_ref[:, pl.ds(j * LANES, width)] = result[j : j + 1, 0:width]


def local(node_coords, tet_nodes, bnd_nodes, reaction, load, area_normal):
    elems, count = tet_nodes.shape[1], bnd_nodes.shape[0]
    tet_rows = -(-elems // 1024) * 8
    length = 4 * tet_rows * LANES
    dma = pltpu.SemaphoreType.DMA
    sol, demag = pl.pallas_call(
        full_kernel,
        out_shape=(
            jax.ShapeDtypeStruct((8, LANES), F32),
            jax.ShapeDtypeStruct((1, count), F32),
        ),
        in_specs=[VMEM] * 6,
        out_specs=(VMEM,) * 2,
        scratch_shapes=[
            pltpu.VMEM((4, tet_rows, LANES), jnp.int32),
            pltpu.VMEM((12, 8, LANES), F32),
            pltpu.VMEM((ITERS, 12, 8, LANES), F32),
            pltpu.VMEM((HALF, length), BF16),
            pltpu.VMEM((32, length), BF16),
            pltpu.VMEM((16, LANES), F32),
            pltpu.VMEM((10, tet_rows, LANES), F32),
            pltpu.VMEM((4, tet_rows, LANES), F32),
            pltpu.VMEM((8, LANES), jnp.int32),
            pltpu.VMEM((8, LANES), jnp.int32),
            pltpu.VMEM((SLOTS, SLOTS), BF16),
            pltpu.VMEM((16, 8, SLOTS), F32),
            pltpu.VMEM((16, 16, LANES), F32),
            pltpu.VMEM((8, 8, WIDE), F32),
            pltpu.VMEM((8, WIDE), F32),
            pltpu.VMEM((2, 64, 18 * WIDE), BF16),
            pltpu.VMEM((9, 2, WIDE, 64), BF16),
            pltpu.VMEM((9, 8, LANES), F32),
            pltpu.VMEM((8, 8, LANES), F32),
            pltpu.VMEM((8, 8, LANES), F32),
            pltpu.VMEM((ITERS, 8, 8, LANES), F32),
            pltpu.VMEM((ITERS, 16, 8, LANES), F32),
            dma((1 + ITERS, 2)), dma((1 + ITERS, 2)),
            dma((ITERS, 22)), dma((ITERS, 22)),
            dma((2, 8)), dma((2, 8)),
            dma((7,)), dma((7,)),
            dma((8,)), dma(()),
            dma((7,)), dma((7,)),
            dma(()), dma((8,)),
        ],
        compiler_params=pltpu.CompilerParams(collective_id=0, has_side_effects=True, vmem_limit_bytes=60 << 20),
        name="full",
    )(tet_nodes, node_coords, bnd_nodes.reshape(1, count), area_normal,
      reaction.reshape(8, LANES), load.reshape(8, LANES))
    return sol.reshape(-1), demag.reshape(-1)


def solution(mesh):
    placed = (
        P(None, ("row", "col")),
        P(None, ("row", "col")),
        P(("row", "col")),
        P(("row", "col")),
        P(("row", "col")),
        P(None, ("row", "col")),
    )
    return jax.shard_map(
        local,
        mesh=mesh,
        in_specs=placed,
        out_specs=(P(("row", "col")), P(("row", "col"))),
        check_vma=False,
    )
```

```python
import functools
import math

import jax
import jax.numpy as jnp
from jax import lax
from jax.experimental import pallas as pl
from jax.experimental.pallas import tpu as pltpu
from jax.sharding import PartitionSpec as P

ITERS = 3
LANES = 128
SLOTS = 512
F32 = jnp.float32
BF16 = jnp.bfloat16
MESH = pl.DeviceIdType.MESH
VMEM = pl.BlockSpec(memory_space=pltpu.VMEM)
CHUNK = 7168
QS = 16
WIDE = 256
HALF = 64
MAIN = 4 * 4 * (QS - 1)
BLOCK = 240
UNROLL = 18
PAIRS = [(a, b) for a in range(4) for b in range(a, 4)]


def place():
    row, col = lax.axis_index("row"), lax.axis_index("col")
    z_hi, y = row // 4, row % 4
    z_lo, g = col // 8, col % 8
    return row, col, z_hi, y, z_lo, g


def peers():
    row, col, z_hi, y, z_lo, g = place()
    out = [(row, z_lo * 8 + (g + j) % 8) for j in range(1, 8)]
    plane = (z_hi * 2 + z_lo) * 4 + y
    for j in range(1, 16):
        other = (plane + j) % 16
        z = other // 4
        out.append(((z // 2) * 4 + other % 4, (z % 2) * 8 + g))
    return out


def lane_pick(table, low):
    return jnp.take_along_axis(table, low, axis=1, mode="promise_in_bounds")


def pick(rows, ids):
    low = ids & (LANES - 1)
    high = ids >> 7
    out = jnp.zeros(ids.shape, F32)
    for r, row in enumerate(rows):
        out = jnp.where(high == r, lane_pick(row, low), out)
    return out


def pieces(v):
    one = v.astype(BF16).astype(F32)
    rest = v - one
    two = rest.astype(BF16).astype(F32)
    return one, two, rest - two


def cross(u, v):
    return (
        u[1] * v[2] - u[2] * v[1],
        u[2] * v[0] - u[0] * v[2],
        u[0] * v[1] - u[1] * v[0],
    )


def dot3(u, v):
    return u[0] * v[0] + u[1] * v[1] + u[2] * v[2]


def full_kernel(
    tet_ref, nc_ref, bnd_ref, an_ref, rea_ref, load_ref,
    sol_ref, out_ref,
    ids, ext_c, ext_v, onehot, spread, folded, stiff, vals, slots, chosen, order,
    source, trace, near, far, rhs, lhs, part, fin, fex,
    red_a, red_b,
    halo_s, halo_r, red_s, red_r, all_s, all_r, near_s, near_r, far_s, far_r,
    fin_s, fin_r, fex_s, fex_r,
):
    row, col, z_hi, y, z_lo, g = place()
    z = z_hi * 2 + z_lo
    others = peers()
    before, after = (row, (col + 15) % 16), (row, (col + 1) % 16)
    partner = (row, (1 - z_lo) * 8 + g)
    column = [((row + j) % 8, col) for j in range(1, 8)]
    keeper = (col % 8, (1 - col // 8) * 15)
    at_end = col % 15 == 0
    helped = row + (1 - col // 15) * 8
    helpers = [(r, helped) for r in range(8)]
    elems = tet_ref.shape[1]
    count = bnd_ref.shape[1]
    tet_rows = ids.shape[1]

    fex[...] = jnp.zeros(fex.shape, F32)
    folded[...] = jnp.zeros(folded.shape, F32)
    part[...] = jnp.zeros(part.shape, F32)

    barrier = pltpu.get_barrier_semaphore()
    greeted = others + [before, after]
    for who in greeted:
        pl.semaphore_signal(barrier, inc=1, device_id=who, device_id_type=MESH)

    def remote(src, dst, ssem, rsem, who):
        return pltpu.make_async_remote_copy(
            src_ref=src, dst_ref=dst, send_sem=ssem, recv_sem=rsem,
            device_id=who, device_id_type=MESH,
        )

    def send(*args):
        copy = remote(*args)
        copy.start()
        return copy

    def halo(buf, k):
        return [
            send(buf.at[pl.ds(2, 2)], buf.at[pl.ds(10, 2)], halo_s.at[k, 0], halo_r.at[k, 0], before),
            send(buf.at[pl.ds(8, 2)], buf.at[pl.ds(0, 2)], halo_s.at[k, 1], halo_r.at[k, 1], after),
        ]

    shared = (8, 12)

    def share(buf, k):
        tile = buf.at[col, pl.ds(0, shared[k])]
        return [send(tile, tile, all_s.at[k, j], all_r.at[k, j], others[j]) for j in range(7)]

    def share_on(buf, k):
        tiles = buf.at[pl.ds(z_lo * 8, 8), pl.ds(0, shared[k])]
        return [send(tiles, tiles, all_s.at[k, 7], all_r.at[k, 7], partner)]

    def finish(copies):
        for copy in copies:
            copy.wait()

    groups = ((red_a, g, 8, 0), (red_b, z * 4 + y, 16, 7))

    def reduce_stage(rows, k, stage):
        buf, mine, size, first = groups[stage]
        buf[k, mine, pl.ds(0, 2), :] = rows
        tile = buf.at[k, mine, pl.ds(0, 2)]
        return [
            send(tile, tile, red_s.at[k, first + j], red_r.at[k, first + j], others[first + j])
            for j in sorted(range(size - 1), key=lambda j: abs(2 * j - size))
        ]

    def reduce_sum(copies, k, stage):
        finish(copies)
        buf, _, size, _ = groups[stage]
        rows = buf[k, 0, pl.ds(0, 2), :]
        for i in range(1, size):
            rows = rows + buf[k, i, pl.ds(0, 2), :]
        return rows

    def reduce_begin(u, v, k):
        rows = jnp.concatenate([jnp.sum(u, axis=0, keepdims=True), jnp.sum(v, axis=0, keepdims=True)], axis=0)
        return reduce_stage(rows, k, 0)

    def reduce_on(copies, k, stage):
        return reduce_stage(reduce_sum(copies, k, stage), k, stage + 1)

    def reduce_end(copies, k):
        rows = jnp.sum(reduce_sum(copies, k, 1), axis=1, keepdims=True)
        return rows[0:1], rows[1:2]

    for s in range(8):
        for k in range(3):
            ext_c[2 + s, pl.ds(k, 1), :] = nc_ref[pl.ds(k, 1), pl.ds(s * LANES, LANES)]
        ext_c[2 + s, pl.ds(3, 5), :] = jnp.zeros((5, LANES), F32)

    slots[...] = jnp.full(slots.shape, -1, jnp.int32)
    for j in range(SLOTS // LANES):
        width = min(LANES, count - j * LANES)
        slots[pl.ds(j, 1), pl.ds(0, width)] = bnd_ref[:, pl.ds(j * LANES, width)]
    slot_ids = slots[...]
    live = jnp.where(slot_ids >= 0, 1.0, 0.0)
    tri = lax.broadcasted_iota(jnp.int32, (LANES, LANES), 0) <= lax.broadcasted_iota(jnp.int32, (LANES, LANES), 1)
    tri = jnp.where(tri, 1.0, 0.0).astype(BF16)
    rank = jnp.dot(live.astype(BF16), tri, preferred_element_type=F32) - 1.0
    totals = jnp.sum(live, axis=1, keepdims=True)
    base = jnp.zeros((1, 1), F32)
    bases = []
    for j in range(8):
        bases.append(base)
        base = base + totals[j : j + 1]
    rank = rank + jnp.concatenate(bases, axis=0)
    spot = (rank + jnp.where(rank >= MAIN, 1.0 * (WIDE - MAIN), 0.0)).astype(jnp.int32)
    spot = jnp.where(slot_ids >= 0, spot, -1)
    for j in range(SLOTS // LANES):
        line = jnp.broadcast_to(spot[j : j + 1, :], (SLOTS, LANES))
        hot = jnp.where(line == lax.broadcasted_iota(jnp.int32, (SLOTS, LANES), 0), 1.0, 0.0)
        order[:, pl.ds(j * LANES, LANES)] = hot.astype(BF16)
    tile = source.at[col]
    tile[...] = jnp.zeros((8, SLOTS), F32)
    for j in range(SLOTS // LANES):
        tile[pl.ds(0, 1), pl.ds(j * LANES, LANES)] = (slot_ids[j : j + 1, :] + 1).astype(F32)
    for k in range(3):
        tile[pl.ds(1 + k, 1), pl.ds(0, count)] = an_ref[pl.ds(k, 1), :]
    one, two, three = pieces(tile[...])
    stacked = jnp.concatenate([one, two, three, jnp.zeros((8, SLOTS), F32)], axis=0).astype(BF16)
    moved = lax.dot_general(stacked, order[...], (((1,), (1,)), ((), ())), preferred_element_type=F32)
    moved = moved[0:8] + moved[8:16] + moved[16:24]
    chosen[...] = jnp.full(chosen.shape, -1, jnp.int32)
    for j in range(SLOTS // LANES):
        chosen[pl.ds(j, 1), :] = moved[0:1, j * LANES : (j + 1) * LANES].astype(jnp.int32) - 1
    nodes = chosen[...]
    tile[pl.ds(3, 3), :] = moved[1:4]
    for k in range(3):
        tables = [jnp.broadcast_to(ext_c[2 + s, pl.ds(k, 1), :], (8, LANES)) for s in range(8)]
        where = pick(tables, nodes)
        for j in range(SLOTS // LANES):
            tile[pl.ds(k, 1), pl.ds(j * LANES, LANES)] = where[j : j + 1, :]
    near[row] = tile[:, 0:WIDE]

    pl.semaphore_wait(barrier, len(greeted))
    coords_sent = halo(ext_c, 0)
    static_sent = share(source, 0)

    def send_targets():
        for j in range(7):
            send(near.at[row], near.at[row], near_s.at[j], near_r.at[j], column[j])

        @pl.when(at_end)
        def _():
            for r in range(8):
                remote(tile.at[:, pl.ds(WIDE, WIDE)], far, far_s.at[r], far_r, helpers[r]).start()

    full = elems // LANES
    for a in range(4):
        ids[a, pl.ds(full // 8 * 8, tet_rows - full // 8 * 8), :] = jnp.full(
            (tet_rows - full // 8 * 8, LANES), -1, jnp.int32)
        for j in range(full):
            ids[a, pl.ds(j, 1), :] = tet_ref[pl.ds(a, 1), pl.ds(j * LANES, LANES)]
        rest = elems - full * LANES
        if rest:
            ids[a, pl.ds(full, 1), pl.ds(0, rest)] = tet_ref[pl.ds(a, 1), pl.ds(full * LANES, rest)]

    def build(q, carry):
        lane = lax.broadcasted_iota(jnp.int32, (HALF, LANES), 0)
        for a in range(4):
            low = jnp.broadcast_to(ids[a, pl.ds(q, 1), :] & (HALF - 1), (HALF, LANES))
            hot = jnp.where(low == lane, 1.0, 0.0).astype(BF16)
            onehot[:, pl.ds(pl.multiple_of((q * 4 + a) * LANES, LANES), LANES)] = hot
        return carry

    lax.fori_loop(0, tet_rows, build, 0)

    def node_sums():
        def spread_rows(q, carry):
            level = lax.broadcasted_iota(jnp.int32, (16, LANES), 0) + 4
            for a in range(4):
                high = jnp.broadcast_to(ids[a, pl.ds(q, 1), :] >> 6, (16, LANES))
                val = jnp.broadcast_to(vals[a, pl.ds(q, 1), :], (8, LANES))
                one = val.astype(BF16).astype(F32)
                hit = high == level
                two = val - one
                one, two = [jnp.where(hit, jnp.concatenate([v, v], axis=0), 0.0) for v in (one, two)]
                block = jnp.concatenate([one, two], axis=0)
                spread[:, pl.ds(pl.multiple_of((q * 4 + a) * LANES, LANES), LANES)] = block.astype(BF16)
            return carry

        lax.fori_loop(0, tet_rows, spread_rows, 0, unroll=4)

        def accumulate(i, total):
            at = pl.ds(pl.multiple_of(i * CHUNK, CHUNK), CHUNK)
            return total + lax.dot_general(
                spread[:, at], onehot[:, at], (((1,), (1,)), ((), ())), preferred_element_type=F32)

        total = lax.fori_loop(0, onehot.shape[1] // CHUNK, accumulate, jnp.zeros((32, HALF), F32))
        folded[:, pl.ds(0, HALF)] = total[0:16] + total[16:32]
        even = folded[pl.ds(0, 8, stride=2), :]
        odd = pltpu.roll(folded[pl.ds(1, 8, stride=2), :], HALF, 1)
        return jnp.where(lax.broadcasted_iota(jnp.int32, (8, LANES), 1) < HALF, even, odd)

    finish(coords_sent)

    def shape_elements(i, carry):
        at = pl.ds(pl.multiple_of(i * 8, 8), 8)
        corner = [ids[a, at, :] for a in range(4)]
        spots = []
        for a in range(4):
            low, high = corner[a] & (LANES - 1), corner[a] >> 7
            xyz = [jnp.zeros((8, LANES), F32) for _ in range(3)]
            for r in range(12):
                hit = high == r
                for k in range(3):
                    line = jnp.broadcast_to(ext_c[r, pl.ds(k, 1), :], (8, LANES))
                    xyz[k] = jnp.where(hit, lane_pick(line, low), xyz[k])
            spots.append(xyz)
        edges = [[spots[a][k] - spots[0][k] for k in range(3)] for a in range(1, 4)]
        n1 = cross(edges[1], edges[2])
        n2 = cross(edges[2], edges[0])
        n3 = cross(edges[0], edges[1])
        n0 = tuple(-(n1[k] + n2[k] + n3[k]) for k in range(3))
        present = corner[0] >= 0
        volume = jnp.abs(jnp.where(present, dot3(edges[0], n1), 1.0))
        weight = jnp.where(present, 1.0 / (6.0 * volume), 0.0)
        normals = (n0, n1, n2, n3)
        for e, (a, b) in enumerate(PAIRS):
            value = dot3(normals[a], normals[b]) * weight
            stiff[e, at, :] = value
            if a == b:
                vals[a, at, :] = value
        return carry

    lax.fori_loop(0, tet_rows // 8, shape_elements, 0)
    reaction = rea_ref[...]
    diagonal = reaction + node_sums()

    def apply(field, k, running=None):
        table = ext_v.at[k]
        for s in range(8):
            table[2 + s] = jnp.broadcast_to(field[s : s + 1, :], (8, LANES))
        sent = halo(table, 1 + k)
        if running is not None:
            running.append(reduce_on(running.pop(), k - 1, 0))
        finish(sent)

        def products(i, carry):
            at = pl.ds(pl.multiple_of(i * 8, 8), 8)
            corner = []
            for a in range(4):
                corner.append(pick([table[r] for r in range(12)], ids[a, at, :]))
            sums = [None] * 4
            for e, (a, b) in enumerate(PAIRS):
                value = stiff[e, at, :]
                for m, n in {(a, b), (b, a)}:
                    term = value * corner[n]
                    sums[m] = term if sums[m] is None else sums[m] + term
            for a in range(4):
                vals[a, at, :] = sums[a]
            return carry

        lax.fori_loop(0, tet_rows // 8, products, 0, unroll=True)

        return reaction * field + node_sums()

    r = load_ref[...]
    u = r / diagonal
    w = apply(u, 0)
    x = zz = q = s_ = p = gamma_old = alpha = None
    for k in range(ITERS - 1):
        running = [reduce_begin(r * u, w * u, k)]
        m = w / diagonal
        n = apply(m, k + 1, running)
        gamma, delta = reduce_end(running.pop(), k)
        if k == 0:
            alpha = gamma / delta
            zz, q, s_, p = n, m, w, u
            x = alpha * p
        else:
            beta = gamma / gamma_old
            alpha = gamma / (delta - beta * gamma / alpha)
            zz, q, s_, p = n + beta * zz, m + beta * q, w + beta * s_, u + beta * p
            x = x + alpha * p
        r, u, w = r - alpha * s_, u - alpha * q, w - alpha * zz
        gamma_old = gamma
        if k == 0:
            send_targets()
            finish(static_sent)
            static_sent = share_on(source, 0)
    last = ITERS - 1
    running = reduce_begin(r * u, w * u, last)

    for i, part_of in enumerate((x, u, p)):
        tables = [jnp.broadcast_to(part_of[s : s + 1, :], (8, LANES)) for s in range(8)]
        trace[col, pl.ds(4 * i, 4), :] = pick(tables, nodes)[0:4]
    trace_sent = share(trace, 1)
    running = reduce_on(running, last, 0)

    def split_target(b, tile, first):
        t = tile[0:3] - first
        t_one, t_two, t_three = pieces(t)
        q_one, q_two, q_three = pieces(dot3((t[0:1], t[1:2], t[2:3]), (t[0:1], t[1:2], t[2:3])))
        none3, none1 = jnp.zeros((3, WIDE), F32), jnp.zeros((1, WIDE), F32)
        unit = jnp.ones((1, WIDE), F32)
        blocks_d, blocks_n = [], []
        for piece, lead in ((t_one, 1), (t_two, 0), (t_three, 0), (t_one, 1), (t_two, 0), (t_one, 1)):
            flag = unit if lead else none1
            blocks_d += [-2.0 * piece, none3, flag, none1]
            blocks_n += [none3, piece, none1, -flag]
        blocks_d += [q_one, q_two, q_three] + [none1] * 13
        blocks_n += [none1] * 16
        fill = jnp.zeros((64, WIDE), F32)
        for i, blocks in enumerate((blocks_d, blocks_n)):
            lhs[b, i] = jnp.concatenate(blocks + [fill], axis=0).T[:, 0:64].astype(BF16)

    finish(static_sent)
    for j in range(7):
        remote(near.at[row], near.at[row], near_s.at[j], near_r.at[j], column[j]).wait()
    remote(far, far, far_s.at[0], far_r, keeper).wait_recv()

    @pl.when(at_end)
    def _():
        for r in range(8):
            remote(tile.at[:, pl.ds(WIDE, WIDE)], far, far_s.at[r], far_r, helpers[r]).wait_send()

    own_first = near[row][0:3, 0:1]
    far_first = far[0:3, 0:1]

    def split_near(b, carry):
        split_target(b, near[b], own_first)
        return carry

    lax.fori_loop(0, 8, split_near, 0)
    split_target(8, far[...], far_first)

    finish(trace_sent)
    trace_sent = share_on(trace, 1)
    gamma, delta = reduce_end(running, last)
    beta = gamma / gamma_old
    alpha = gamma / (delta - beta * gamma / alpha)
    x = x + alpha * (u + beta * p)
    sol_ref[...] = x
    tables = [jnp.broadcast_to(x[s : s + 1, :], (8, LANES)) for s in range(8)]
    own_trace = pick(tables, slot_ids)
    finish(trace_sent)

    def whole_trace(c):
        return trace[c, pl.ds(0, 4), :] + alpha * (trace[c, pl.ds(4, 4), :] + beta * trace[c, pl.ds(8, 4), :])

    def split_sources(kind, first):
        unit = jnp.where(lax.broadcasted_iota(jnp.int32, (8, WIDE), 0) < 3, 1.0, 0.0).astype(F32)

        def put(i, tile, tr):
            s = tile[0:3] - first
            w = tile[3:6] * tr
            sx, wx = [s[k : k + 1] for k in range(3)], [w[k : k + 1] for k in range(3)]
            data = jnp.concatenate([s, w, dot3(sx, sx) + 0.25, dot3(sx, wx)], axis=0)
            one, two, three = pieces(data)
            block = jnp.concatenate([one, one, one, two, two, three, unit, jnp.zeros((8, WIDE), F32)], axis=0)
            rhs[kind, :, pl.ds(pl.multiple_of(i * WIDE, WIDE), WIDE)] = block.astype(BF16)

        def each(c, carry):
            tr = whole_trace(c)
            put(c, source[c, :, pl.ds(0, WIDE)], jnp.concatenate([tr[0:1], tr[1:2]], axis=1))
            return carry

        lax.fori_loop(0, 16, each, 0)
        for i, c in ((16, 0), (17, 15)):
            tr = whole_trace(c)
            put(i, source[c, :, pl.ds(WIDE, WIDE)], jnp.concatenate([tr[2:3], tr[3:4]], axis=1))

    def pair_sums(b, kind):
        parts = []
        for low, high in ((0, BLOCK),):
            left_d, left_n = lhs[b, 0, low:high, :], lhs[b, 1, low:high, :]

            def some(i, total):
                for u in range(UNROLL):
                    right = rhs[kind, :, pl.ds(pl.multiple_of((i * UNROLL + u) * WIDE, WIDE), WIDE)]
                    d = jnp.dot(left_d, right, preferred_element_type=F32)
                    n = jnp.dot(left_n, right, preferred_element_type=F32)
                    inv = lax.rsqrt(d)
                    c = (n * inv) * (inv * inv)
                    total = total + (c[:, 0:LANES] + c[:, LANES:WIDE])
                return total

            parts.append(lax.fori_loop(0, 18 // UNROLL, some, jnp.zeros((high - low, LANES), F32)))
        parts.append(jnp.zeros((WIDE - BLOCK, LANES), F32))
        return jnp.sum(jnp.concatenate(parts, axis=0).T, axis=0, keepdims=True)

    def keep(ref, sums):
        ref[pl.ds(0, 1), :] = sums[:, 0:LANES]
        ref[pl.ds(1, 1), :] = sums[:, LANES:WIDE]

    split_sources(0, far_first)
    split_sources(1, own_first)

    def one_block(j, carry):
        other = (row + j) % 8
        b = jnp.where(j == 0, 8, other)
        keep(part.at[b], pair_sums(b, jnp.minimum(j, 1)))

        @pl.when(j == 0)
        def _():
            remote(part.at[8], fex.at[row], fex_s, fex_r.at[row], keeper).start()

        @pl.when(jnp.logical_and(j > 0, j < 8))
        def _():
            remote(part.at[other], fin.at[row], fin_s.at[j - 1], fin_r.at[j - 1], (other, col)).start()

        return carry

    lax.fori_loop(0, 9, one_block, 0)
    fin[row] = part[row]
    remote(part.at[8], fex.at[row], fex_s, fex_r.at[row], keeper).wait_send()
    for j in range(7):
        remote(part.at[row], fin.at[row], fin_s.at[j], fin_r.at[j], column[j]).wait()

    @pl.when(at_end)
    def _():
        for r in range(8):
            remote(part.at[8], fex.at[r], fex_s, fex_r.at[r], keeper).wait_recv()

    total, more = fin[0], fex[0]
    for r in range(1, 8):
        total, more = total + fin[r], more + fex[r]
    tables = [jnp.broadcast_to(v[j : j + 1, :], (8, LANES)) for v in (total, more) for j in range(2)]
    result = live * (-0.5 * own_trace + (0.25 / math.pi) * pick(tables, spot))
    for j in range(SLOTS // LANES):
        width = min(LANES, count - j * LANES)
        out_ref[:, pl.ds(j * LANES, width)] = result[j : j + 1, 0:width]


def local(node_coords, tet_nodes, bnd_nodes, reaction, load, area_normal):
    elems, count = tet_nodes.shape[1], bnd_nodes.shape[0]
    tet_rows = -(-elems // 1024) * 8
    length = 4 * tet_rows * LANES
    dma = pltpu.SemaphoreType.DMA
    sol, demag = pl.pallas_call(
        full_kernel,
        out_shape=(
            jax.ShapeDtypeStruct((8, LANES), F32),
            jax.ShapeDtypeStruct((1, count), F32),
        ),
        in_specs=[VMEM] * 6,
        out_specs=(VMEM,) * 2,
        scratch_shapes=[
            pltpu.VMEM((4, tet_rows, LANES), jnp.int32),
            pltpu.VMEM((12, 8, LANES), F32),
            pltpu.VMEM((ITERS, 12, 8, LANES), F32),
            pltpu.VMEM((HALF, length), BF16),
            pltpu.VMEM((32, length), BF16),
            pltpu.VMEM((16, LANES), F32),
            pltpu.VMEM((10, tet_rows, LANES), F32),
            pltpu.VMEM((4, tet_rows, LANES), F32),
            pltpu.VMEM((8, LANES), jnp.int32),
            pltpu.VMEM((8, LANES), jnp.int32),
            pltpu.VMEM((SLOTS, SLOTS), BF16),
            pltpu.VMEM((16, 8, SLOTS), F32),
            pltpu.VMEM((16, 16, LANES), F32),
            pltpu.VMEM((8, 8, WIDE), F32),
            pltpu.VMEM((8, WIDE), F32),
            pltpu.VMEM((2, 64, 18 * WIDE), BF16),
            pltpu.VMEM((9, 2, WIDE, 64), BF16),
            pltpu.VMEM((9, 8, LANES), F32),
            pltpu.VMEM((8, 8, LANES), F32),
            pltpu.VMEM((8, 8, LANES), F32),
            pltpu.VMEM((ITERS, 8, 8, LANES), F32),
            pltpu.VMEM((ITERS, 16, 8, LANES), F32),
            dma((1 + ITERS, 2)), dma((1 + ITERS, 2)),
            dma((ITERS, 22)), dma((ITERS, 22)),
            dma((2, 8)), dma((2, 8)),
            dma((7,)), dma((7,)),
            dma((8,)), dma(()),
            dma((7,)), dma((7,)),
            dma(()), dma((8,)),
        ],
        compiler_params=pltpu.CompilerParams(collective_id=0, has_side_effects=True, vmem_limit_bytes=60 << 20),
        name="full",
    )(tet_nodes, node_coords, bnd_nodes.reshape(1, count), area_normal,
      reaction.reshape(8, LANES), load.reshape(8, LANES))
    return sol.reshape(-1), demag.reshape(-1)


def solution(mesh):
    placed = (
        P(None, ("row", "col")),
        P(None, ("row", "col")),
        P(("row", "col")),
        P(("row", "col")),
        P(("row", "col")),
        P(None, ("row", "col")),
    )
    return jax.shard_map(
        local,
        mesh=mesh,
        in_specs=placed,
        out_specs=(P(("row", "col")), P(("row", "col"))),
        check_vma=False,
    )
```
